32 devices in a mesh: dp: 4 (over y, core), mp: 8 (over z, x).
Axes of the slice: x: 2, y: 2, z: 4, core: 2. Of those that a mesh axis runs over, the one named last changes fastest.
Arguments:
- inputs: bfloat16 [2048, 16384], P('dp', 'mp'), may hold values from -6 to 6
- out_grad: bfloat16 [2048, 16384], P('dp', 'mp'), may hold values from -6 to 6
- w_up: bfloat16 [2, 256, 256, 256], P(None, 'mp'), may hold values from -0.25 to 0.25
- w_down: bfloat16 [2, 256, 256, 256], P(None, 'mp'), may hold values from -0.125 to 0.125
- partners: int32 [2, 256], P(None, 'mp'), may hold values from 0 to 63, as said below
Outputs:
- outputs: bfloat16 [2048, 16384], P('dp', 'mp')
- in_grad: bfloat16 [2048, 16384], P('dp', 'mp')
- up_grad: float32 [2, 256, 256, 256], P(None, 'mp', 'dp')
- down_grad: float32 [2, 256, 256, 256], P(None, 'mp', 'dp')
The draws below stay inside these ranges and needn't reach their ends.
Inputs may be any that keep to these rules, and one draw needn't show every extreme that they name: partners[s, c] = (c // 4) XOR m, where m is 0 or a power of two below 64; the two slots of a column name different blocks.
All inputs are finite; a program needn't handle non-finite values.
Results may differ from the reference program's by a relative error of at most 0.0056.
Values may be sent and summed in bfloat16 or wider, within the bound.
No kernel may reach another device: no remote copies, remote signals or barrier semaphores. Data moves between devices by JAX's collectives and lax.ppermute only.
A program may use at most 256 MiB of HBM per device.

```python
import jax
import jax.numpy as jnp
from jax import lax

D = 16384
BS = 256
SLOTS = 2
TOKENS = 2048
NBI = 64
NBH = 256
HR = 4
N_MP = 8


def draw_partners(key, part):
    bit_count = NBI.bit_length() - 1
    first_key, second_key = jax.random.split(key)
    offset = jax.random.randint(first_key, (), 0, bit_count, dtype=jnp.int32)
    extra_step = jax.random.randint(second_key, (NBH,), 0, bit_count, dtype=jnp.int32)
    column = jnp.arange(NBH, dtype=jnp.int32)
    row_index = column // HR
    first_bit = (column + offset) % bit_count
    second_bit = (first_bit + 1 + extra_step) % bit_count
    first_mask = jnp.left_shift(jnp.ones_like(first_bit), first_bit)
    second_mask = jnp.where(extra_step == bit_count - 1, jnp.zeros_like(second_bit), jnp.left_shift(jnp.ones_like(second_bit), second_bit))
    first_slot = jnp.bitwise_xor(row_index, first_mask)
    second_slot = jnp.bitwise_xor(row_index, second_mask)
    return jnp.stack([first_slot, second_slot]).astype(jnp.int32)


def steps_of(stream_key, extent, pieces, low, high):
    gain, own = 1.0, jax.random.fold_in(stream_key, 6)
    for position, parts in pieces:
        draws = jnp.exp(jax.random.uniform(jax.random.fold_in(own, position), (parts,), jnp.float32, low / len(pieces), high / len(pieces)))
        gain = gain * jnp.repeat(draws, extent[position] // parts).reshape([-1 if axis == position else 1 for axis in range(len(extent))])
    return gain


def centred(key, shape, deviation, reach, pieces=(), kind=jnp.bfloat16):
    values = jax.random.normal(key, shape, jnp.float32) * deviation
    if len(pieces) > 0:
        values = steps_of(key, shape, pieces, -0.22, 0.18) * values
    return jnp.clip(values, min=-reach, max=reach).astype(kind)


def setup_inputs(seed: int = 0) -> dict:
    arg_keys = jax.random.split(jax.random.key(seed), 6)
    return {
        "inputs": centred(arg_keys[0], (TOKENS, D), 1.0, 6.0, ((0, 4), (1, 8))),
        "out_grad": centred(arg_keys[1], (TOKENS, D), 1.0, 6.0, ((0, 4), (1, 8))),
        "w_up": centred(arg_keys[2], (SLOTS, NBH, BS, BS), (SLOTS * BS) ** -0.5, 0.25, ((1, 8),)),
        "w_down": centred(arg_keys[3], (SLOTS, NBH, BS, BS), (SLOTS * HR * BS) ** -0.5, 0.125, ((1, 8),)),
        "partners": draw_partners(jax.random.fold_in(arg_keys[5], 71), 0),
    }


def gelu_pair(hidden):
    erf_part = jax.scipy.special.erf(hidden * 0.7071067811865476)
    value = 0.5 * hidden * (1.0 + erf_part)
    slope = 0.5 * (1.0 + erf_part) + hidden * jnp.exp(-0.5 * hidden * hidden) * 0.3989422804014327
    return value, slope


def reference(inputs, out_grad, w_up, w_down, partners):
    in_blocks = inputs.reshape(TOKENS, NBI, BS).transpose(1, 0, 2)
    grad_blocks = out_grad.reshape(TOKENS, NBI, BS).transpose(1, 0, 2)
    cols_dev = NBH // N_MP
    blocks_dev = NBI // N_MP

    def column_step(carry, column):
        out_total, in_total, out_remote, in_remote = carry
        owner = column // cols_dev
        chosen = partners[:, column]
        from_inputs = in_blocks[chosen]
        from_grads = grad_blocks[chosen]
        up_pair = w_up[:, column]
        down_pair = w_down[:, column]
        pre_act = jnp.dot(from_inputs[0], up_pair[0], preferred_element_type=jnp.float32)
        pre_act = pre_act + jnp.dot(from_inputs[1], up_pair[1], preferred_element_type=jnp.float32)
        value, slope = gelu_pair(pre_act)
        activated = value.astype(jnp.bfloat16)
        hidden_grad = jnp.dot(from_grads[0], down_pair[0].T, preferred_element_type=jnp.float32)
        hidden_grad = hidden_grad + jnp.dot(from_grads[1], down_pair[1].T, preferred_element_type=jnp.float32)
        pre_grad = (hidden_grad * slope).astype(jnp.bfloat16)
        up_list = []
        down_list = []
        for slot in range(SLOTS):
            target = chosen[slot]
            is_local = (target // blocks_dev) == owner
            out_term = jnp.dot(activated, down_pair[slot], preferred_element_type=jnp.float32)
            in_term = jnp.dot(pre_grad, up_pair[slot].T, preferred_element_type=jnp.float32)
            zero_term = jnp.zeros_like(out_term)
            out_total = out_total.at[target].add(jnp.where(is_local, out_term, zero_term))
            in_total = in_total.at[target].add(jnp.where(is_local, in_term, zero_term))
            out_remote = out_remote.at[target].add(jnp.where(is_local, zero_term, out_term))
            in_remote = in_remote.at[target].add(jnp.where(is_local, zero_term, in_term))
            up_list.append(jnp.dot(from_inputs[slot].T, pre_grad, preferred_element_type=jnp.float32))
            down_list.append(jnp.dot(activated.T, from_grads[slot], preferred_element_type=jnp.float32))
        return (out_total, in_total, out_remote, in_remote), (jnp.stack(up_list), jnp.stack(down_list))

    def device_step(carry, device):
        out_total, in_total = carry
        empty = jnp.zeros((NBI, TOKENS, BS), jnp.float32)
        columns = device * cols_dev + jnp.arange(cols_dev, dtype=jnp.int32)
        (out_total, in_total, out_remote, in_remote), grads = lax.scan(
            column_step, (out_total, in_total, empty, empty), columns)
        out_rounded = lax.optimization_barrier(out_remote.astype(jnp.bfloat16))
        in_rounded = lax.optimization_barrier(in_remote.astype(jnp.bfloat16))
        out_total = out_total + out_rounded.astype(jnp.float32)
        in_total = in_total + in_rounded.astype(jnp.float32)
        return (out_total, in_total), grads

    start = jnp.zeros((NBI, TOKENS, BS), jnp.float32)
    (out_total, in_total), (up_cols, down_cols) = lax.scan(
        device_step, (start, start), jnp.arange(N_MP, dtype=jnp.int32))
    up_cols = up_cols.reshape(NBH, SLOTS, BS, BS)
    down_cols = down_cols.reshape(NBH, SLOTS, BS, BS)
    outputs = out_total.transpose(1, 0, 2).reshape(TOKENS, D).astype(jnp.bfloat16)
    in_grad = in_total.transpose(1, 0, 2).reshape(TOKENS, D).astype(jnp.bfloat16)
    return outputs, in_grad, up_cols.transpose(1, 0, 2, 3), down_cols.transpose(1, 0, 2, 3)
```

```python
import functools

import jax
import jax.numpy as jnp
from jax import lax
from jax.experimental import pallas as pl
from jax.experimental.pallas import tpu as pltpu
from jax.sharding import PartitionSpec as P


GROUPS = 2


def partner(value, axis, distance):
    mask = 2**distance
    pairs = [(source, source ^ mask) for source in range(lax.axis_size(axis))]
    return lax.ppermute(value, axis, pairs)


def gelu_pair(hidden):
    erf_part = lax.erf(hidden * 0.7071067811865476)
    value = 0.5 * hidden * (1.0 + erf_part)
    slope = 0.5 * (1.0 + erf_part) + hidden * jnp.exp(-0.5 * hidden * hidden) * 0.3989422804014327
    return value, slope


def dot_nn(left, right):
    return lax.dot_general(left, right, (((1,), (0,)), ((), ())), preferred_element_type=jnp.float32)


def dot_nt(left, right):
    return lax.dot_general(left, right, (((1,), (1,)), ((), ())), preferred_element_type=jnp.float32)


def dot_tn(left, right):
    return lax.dot_general(left, right, (((0,), (0,)), ((), ())), preferred_element_type=jnp.float32)


def main_body(dims, slots_ref, parity_ref, *refs):
    local, bits, rows, width, _, halves, _, has_prior = dims
    x_hbm, g_hbm = refs[0], refs[1]
    arrived = refs[2 : 2 + bits]
    at = 2 + bits
    prior = refs[at] if has_prior else None
    at += int(has_prior)
    up_ref, down_ref = refs[at], refs[at + 1]
    acc_hbm = refs[at + 2]
    sent = refs[at + 3 : at + 3 + bits]
    keep_ref, send_ref = refs[at + 3 + bits], refs[at + 4 + bits]
    cand, acc, stage, square, in_sems, acc_sems, out_sems = refs[at + 5 + bits :]
    step = pl.program_id(0)
    last = pl.num_programs(0) - 1

    def loads():
        copies = []
        for kind, source in enumerate((x_hbm, g_hbm)):
            for block in range(local):
                view = source.at[:, pl.ds(block * width, width)]
                copies.append((view, cand.at[kind, block]))
        for kind in range(2):
            for bit in range(bits):
                for row in range(rows):
                    view = arrived[bit].at[kind, :, pl.ds(row * width, width)]
                    copies.append((view, cand.at[kind, local + bit * rows + row]))
        return [pltpu.make_async_copy(a, b, in_sems.at[i]) for i, (a, b) in enumerate(copies)]

    def acc_copy(store):
        copies = []
        for kind in range(2):
            for block in range(local):
                index = kind * local + block
                far = acc_hbm if store else prior
                ends = (acc.at[kind, block], far.at[kind, block])
                ends = ends if store else ends[::-1]
                copies.append(pltpu.make_async_copy(*ends, acc_sems.at[index]))
        return copies

    @pl.when(step == 0)
    def _():
        for copy in loads():
            copy.start()
        if has_prior:
            for copy in acc_copy(False):
                copy.start()
        start = local if has_prior else 0
        tokens = acc.shape[2]
        for kind in range(2):

            @pl.loop(start, acc.shape[1])
            def _(slot):
                acc[kind, slot] = jnp.zeros((tokens, width), jnp.float32)

        if has_prior:
            for copy in acc_copy(False):
                copy.wait()
        for copy in loads():
            copy.wait()

    first_slot = slots_ref[step]
    second_slot = slots_ref[pl.num_programs(0) + step]
    slots = (first_slot, second_slot)
    pre_act = dot_nn(cand[0, first_slot], up_ref[0, 0]) + dot_nn(cand[0, second_slot], up_ref[1, 0])
    value, slope = gelu_pair(pre_act)
    activated = value.astype(jnp.bfloat16)
    hidden_grad = dot_nt(cand[1, first_slot], down_ref[0, 0])
    hidden_grad = hidden_grad + dot_nt(cand[1, second_slot], down_ref[1, 0])
    pre_grad = (hidden_grad * slope).astype(jnp.bfloat16)
    parity = parity_ref[0]
    piece = width // (2 * halves)
    for index, slot in enumerate(slots):
        acc[0, slot] += dot_nn(activated, down_ref[index, 0])
        acc[1, slot] += dot_nt(pre_grad, up_ref[index, 0])
        for which, grad in enumerate(
            (dot_tn(cand[0, slot], pre_grad), dot_tn(activated, cand[1, slot]))
        ):
            square[which] = grad
            for half in range(halves):
                own = pl.multiple_of((2 * half + parity) * piece, piece)
                other = pl.multiple_of((2 * half + 1 - parity) * piece, piece)
                keep_ref[0, half, which, index] = square[which, pl.ds(own, piece), :]
                send_ref[0, half, which, index] = square[which, pl.ds(other, piece), :]

    @pl.when(step == last)
    def _():
        for copy in acc_copy(True):
            copy.start()
        for bit in range(bits):
            for kind in range(2):
                for row in range(rows):
                    total = acc[kind, local + bit * rows + row]
                    stage[bit, kind, :, pl.ds(row * width, width)] = total.astype(jnp.bfloat16)
            pltpu.make_async_copy(stage.at[bit], sent[bit], out_sems.at[bit]).start()
        for bit in range(bits):
            pltpu.make_async_copy(stage.at[bit], sent[bit], out_sems.at[bit]).wait()
        for copy in acc_copy(True):
            copy.wait()


def main_call(group, rows, slots, parity, inputs, out_grad, arrived, prior, w_up, w_down, halves):
    tokens, features = inputs.shape
    slot_kinds, columns, width, _ = w_up.shape
    local = features // width
    bits = len(arrived)
    cols = columns * rows // local
    slot_count = local + bits * rows
    first = group * cols
    has_prior = prior is not None
    piece = width // (2 * halves)
    dims = (local, bits, rows, width, slot_count, halves, first, has_prior)
    anywhere = pl.BlockSpec(memory_space=pl.ANY)
    weight = pl.BlockSpec((slot_kinds, 1, width, width), lambda i, *_: (0, first + i, 0, 0))
    grad_block = pl.BlockSpec((1, halves, 2, slot_kinds, piece, width), lambda i, *_: (i, 0, 0, 0, 0, 0))
    grad_shape = jax.ShapeDtypeStruct((cols, halves, 2, slot_kinds, piece, width), jnp.float32)
    operands = [inputs, out_grad, *arrived] + ([prior] if has_prior else []) + [w_up, w_down]
    pair_flops = 2 * tokens * width * width * 6
    moved = 2 * cols * slot_kinds * width * width * 6 + 12 * tokens * width * slot_count
    return pl.pallas_call(
        functools.partial(main_body, dims),
        grid_spec=pltpu.PrefetchScalarGridSpec(
            num_scalar_prefetch=2,
            grid=(cols,),
            in_specs=[anywhere] * (len(operands) - 2) + [weight, weight],
            out_specs=[anywhere] * (1 + bits) + [grad_block, grad_block],
            scratch_shapes=[
                pltpu.VMEM((2, slot_count, tokens, width), jnp.bfloat16),
                pltpu.VMEM((2, slot_count, tokens, width), jnp.float32),
                pltpu.VMEM((bits, 2, tokens, rows * width), jnp.bfloat16),
                pltpu.VMEM((2, width, width), jnp.float32),
                pltpu.SemaphoreType.DMA((2 * slot_count,)),
                pltpu.SemaphoreType.DMA((2 * local,)),
                pltpu.SemaphoreType.DMA((bits,)),
            ],
        ),
        out_shape=[
            jax.ShapeDtypeStruct((2, local, tokens, width), jnp.float32),
            *[jax.ShapeDtypeStruct((2, tokens, rows * width), jnp.bfloat16)] * bits,
            grad_shape,
            grad_shape,
        ],
        cost_estimate=pl.CostEstimate(
            flops=pair_flops * cols * slot_kinds,
            bytes_accessed=moved,
            transcendentals=2 * cols * tokens * width,
        ),
        compiler_params=pltpu.CompilerParams(
            dimension_semantics=("arbitrary",), vmem_limit_bytes=60 << 20
        ),
        name="columns",
    )(slots, parity, *operands)


def halve_body(parity_ref, keep_ref, recv_ref, kept_ref, send_ref):
    parity = parity_ref[0]
    for half in range(kept_ref.shape[1]):
        own = 2 * half + parity
        other = 2 * half + 1 - parity
        kept_ref[:, half] = keep_ref[:, own] + recv_ref[:, own]
        send_ref[:, half] = keep_ref[:, other] + recv_ref[:, other]


def halve_call(parity, keep, recv):
    cols, halves, pair, slot_kinds, piece, width = keep.shape
    block = cols // 4 if cols % 4 == 0 else cols
    spec = pl.BlockSpec((block, halves, pair, slot_kinds, piece, width), lambda i, *_: (i, 0, 0, 0, 0, 0))
    half_shape = (cols, halves // 2, pair, slot_kinds, piece, width)
    half_spec = pl.BlockSpec((block,) + half_shape[1:], lambda i, *_: (i, 0, 0, 0, 0, 0))
    return pl.pallas_call(
        halve_body,
        grid_spec=pltpu.PrefetchScalarGridSpec(
            num_scalar_prefetch=1,
            grid=(cols // block,),
            in_specs=[spec, spec],
            out_specs=[half_spec, half_spec],
        ),
        out_shape=[jax.ShapeDtypeStruct(half_shape, jnp.float32)] * 2,
        cost_estimate=pl.CostEstimate(flops=keep.size, bytes_accessed=12 * keep.size, transcendentals=0),
        name="halve",
    )(parity, keep, recv)


def grads_body(keep_ref, recv_ref, *refs):
    up_ref, down_ref = refs[-2], refs[-1]
    for which, ref in enumerate((up_ref, down_ref)):
        for slot in range(ref.shape[0]):
            ref[slot] = keep_ref[:, 0, which, slot] + recv_ref[:, 0, which, slot]


def grads_call(group, columns, keep, recv, prior):
    cols, _, pair, slot_kinds, piece, width = keep.shape
    block = cols // 4 if cols % 4 == 0 else cols
    first = group * (cols // block)
    spec = pl.BlockSpec((block, 1, pair, slot_kinds, piece, width), lambda i: (i, 0, 0, 0, 0, 0))
    out_spec = pl.BlockSpec((slot_kinds, block, piece, width), lambda i: (0, first + i, 0, 0))
    out_shape = jax.ShapeDtypeStruct((slot_kinds, columns, piece, width), jnp.float32)
    return pl.pallas_call(
        grads_body,
        grid=(cols // block,),
        in_specs=[spec, spec] + [pl.BlockSpec(memory_space=pl.ANY)] * len(prior),
        out_specs=[out_spec, out_spec],
        out_shape=[out_shape, out_shape],
        input_output_aliases={2 + i: i for i in range(len(prior))},
        cost_estimate=pl.CostEstimate(flops=keep.size, bytes_accessed=12 * keep.size, transcendentals=0),
        name="grads",
    )(keep, recv, *prior)


def total_body(bits, acc_ref, *refs):
    out_refs = refs[-2:]
    for kind in range(2):
        total = acc_ref[kind, 0]
        for bit in range(bits):
            total = total + refs[bit][kind].astype(jnp.float32)
        out_refs[kind][...] = total.astype(jnp.bfloat16)


def total_call(group, rows, acc, arrived, prior):
    _, local, tokens, width = acc.shape
    bits = len(arrived)
    first = group * rows
    acc_spec = pl.BlockSpec((2, 1, tokens, width), lambda i: (0, first + i, 0, 0))
    recv_spec = pl.BlockSpec((2, tokens, width), lambda i: (0, 0, i))
    out_spec = pl.BlockSpec((tokens, width), lambda i: (0, first + i))
    out_shape = jax.ShapeDtypeStruct((tokens, local * width), jnp.bfloat16)
    size = 2 * rows * tokens * width
    return pl.pallas_call(
        functools.partial(total_body, bits),
        grid=(rows,),
        in_specs=[acc_spec] + [recv_spec] * bits + [pl.BlockSpec(memory_space=pl.ANY)] * len(prior),
        out_specs=[out_spec, out_spec],
        out_shape=[out_shape, out_shape],
        input_output_aliases={1 + bits + i: i for i in range(len(prior))},
        cost_estimate=pl.CostEstimate(flops=size * bits, bytes_accessed=(6 + 2 * bits) * size, transcendentals=0),
        name="totals",
    )(acc, *arrived, *prior)


def shards(inputs, out_grad, w_up, w_down, partners):
    _, features = inputs.shape
    _, columns, width, _ = w_up.shape
    local = features // width
    bits = lax.axis_size("mp").bit_length() - 1
    dp_bits = lax.axis_size("dp").bit_length() - 1
    group_count = min(GROUPS, local)
    rows = local // group_count
    cols = columns // group_count
    device = lax.axis_index("mp")
    dp_index = lax.axis_index("dp")

    distance = jnp.bitwise_xor(partners // local, device)
    within = partners % local
    level = jnp.zeros_like(distance)
    for bit in range(1, bits):
        level = level + (distance >= 1 << bit).astype(jnp.int32)
    slot = jnp.where(distance == 0, within, local + level * rows + within % rows)
    parities = [(dp_index // 2**bit % 2).reshape(1).astype(jnp.int32) for bit in range(dp_bits)]

    arrived = []
    for group in range(group_count):
        lanes = slice(group * rows * width, (group + 1) * rows * width)
        pair = jnp.stack([inputs[:, lanes], out_grad[:, lanes]])
        arrived.append([partner(pair, "mp", bit) for bit in range(bits)])

    acc = None
    returned = []
    kept = []
    for group in range(group_count):
        slots = slot[:, group * cols : (group + 1) * cols].reshape(-1)
        acc, *rest = main_call(
            group, rows, slots, parities[0], inputs, out_grad, arrived[group], acc, w_up, w_down,
            2 ** (dp_bits - 1),
        )
        returned.append([partner(rest[bit], "mp", bit) for bit in range(bits)])
        keep, send = rest[bits:]
        for bit in range(1, dp_bits):
            recv = partner(send, "dp", bit - 1)
            keep, send = halve_call(parities[bit], keep, recv)
        kept.append((keep, partner(send, "dp", dp_bits - 1)))

    grads = []
    for group in range(group_count):
        grads = grads_call(group, columns, *kept[group], grads)
    totals = []
    for group in range(group_count):
        totals = total_call(group, rows, acc, returned[group], totals)
    return (*totals, *grads)


def solution(mesh):
    in_specs = (
        P("dp", "mp"),
        P("dp", "mp"),
        P(None, "mp", None, None),
        P(None, "mp", None, None),
        P(None, "mp"),
    )
    out_specs = (P("dp", "mp"), P("dp", "mp"), P(None, "mp", "dp", None), P(None, "mp", "dp", None))

    return jax.shard_map(shards, mesh=mesh, in_specs=in_specs, out_specs=out_specs, check_vma=False)
```

```python
import functools

import jax
import jax.numpy as jnp
from jax import lax
from jax.experimental import pallas as pl
from jax.experimental.pallas import tpu as pltpu
from jax.sharding import PartitionSpec as P


PIECES = 8


def row_groups(local):
    if local < PIECES:
        return [1] * local
    unit = local // PIECES
    sizes = [unit] + [2 * unit] * (PIECES // 2 - 1)
    return sizes + [local - sum(sizes)]


def partner(value, axis, distance):
    mask = 2**distance
    pairs = [(source, source ^ mask) for source in range(lax.axis_size(axis))]
    return lax.ppermute(value, axis, pairs)


def gelu_pair(hidden):
    erf_part = lax.erf(hidden * 0.7071067811865476)
    value = 0.5 * hidden * (1.0 + erf_part)
    slope = 0.5 * (1.0 + erf_part) + hidden * jnp.exp(-0.5 * hidden * hidden) * 0.3989422804014327
    return value, slope


def dot_nn(left, right):
    return lax.dot_general(left, right, (((1,), (0,)), ((), ())), preferred_element_type=jnp.float32)


def dot_nt(left, right):
    return lax.dot_general(left, right, (((1,), (1,)), ((), ())), preferred_element_type=jnp.float32)


def dot_tn(left, right):
    return lax.dot_general(left, right, (((0,), (0,)), ((), ())), preferred_element_type=jnp.float32)


def pack_body(x_ref, g_ref, pair_ref):
    pair_ref[0] = x_ref[...]
    pair_ref[1] = g_ref[...]


def pack_call(start, rows, width, inputs, out_grad):
    tokens = inputs.shape[0]
    column = pl.BlockSpec((tokens, width), lambda i: (0, start + i))
    size = 2 * tokens * rows * width
    return pl.pallas_call(
        pack_body,
        grid=(rows,),
        in_specs=[column, column],
        out_specs=pl.BlockSpec((2, tokens, width), lambda i: (0, 0, i)),
        out_shape=jax.ShapeDtypeStruct((2, tokens, rows * width), inputs.dtype),
        cost_estimate=pl.CostEstimate(flops=0, bytes_accessed=4 * size, transcendentals=0),
        name="pack",
    )(inputs, out_grad)


def main_body(dims, slots_ref, parity_ref, *refs):
    local, bits, rows, width, _, halves, _, has_prior = dims
    x_hbm, g_hbm = refs[0], refs[1]
    arrived = refs[2 : 2 + bits]
    at = 2 + bits
    prior = refs[at] if has_prior else None
    at += int(has_prior)
    up_ref, down_ref = refs[at], refs[at + 1]
    acc_hbm = refs[at + 2]
    sent = refs[at + 3 : at + 3 + bits]
    keep_ref, send_ref = refs[at + 3 + bits], refs[at + 4 + bits]
    cand, acc, stage, square, in_sems, acc_sems, out_sems = refs[at + 5 + bits :]
    step = pl.program_id(0)
    last = pl.num_programs(0) - 1

    def loads():
        copies = []
        for kind, source in enumerate((x_hbm, g_hbm)):
            for block in range(local):
                view = source.at[:, pl.ds(block * width, width)]
                copies.append((view, cand.at[kind, block]))
        for kind in range(2):
            for bit in range(bits):
                for row in range(rows):
                    view = arrived[bit].at[kind, :, pl.ds(row * width, width)]
                    copies.append((view, cand.at[kind, local + bit * rows + row]))
        return [pltpu.make_async_copy(a, b, in_sems.at[i]) for i, (a, b) in enumerate(copies)]

    def acc_copy(store):
        copies = []
        for kind in range(2):
            for block in range(local):
                index = kind * local + block
                far = acc_hbm if store else prior
                ends = (acc.at[kind, block], far.at[kind, block])
                ends = ends if store else ends[::-1]
                copies.append(pltpu.make_async_copy(*ends, acc_sems.at[index]))
        return copies

    @pl.when(step == 0)
    def _():
        for copy in loads():
            copy.start()
        if has_prior:
            for copy in acc_copy(False):
                copy.start()
        start = local if has_prior else 0
        tokens = acc.shape[2]
        for kind in range(2):

            @pl.loop(start, acc.shape[1])
            def _(slot):
                acc[kind, slot] = jnp.zeros((tokens, width), jnp.float32)

        if has_prior:
            for copy in acc_copy(False):
                copy.wait()
        for copy in loads():
            copy.wait()

    first_slot = slots_ref[step]
    second_slot = slots_ref[pl.num_programs(0) + step]
    slots = (first_slot, second_slot)
    pre_act = dot_nn(cand[0, first_slot], up_ref[0, 0]) + dot_nn(cand[0, second_slot], up_ref[1, 0])
    value, slope = gelu_pair(pre_act)
    activated = value.astype(jnp.bfloat16)
    hidden_grad = dot_nt(cand[1, first_slot], down_ref[0, 0])
    hidden_grad = hidden_grad + dot_nt(cand[1, second_slot], down_ref[1, 0])
    pre_grad = (hidden_grad * slope).astype(jnp.bfloat16)
    parity = parity_ref[0]
    piece = width // (2 * halves)
    for index, slot in enumerate(slots):
        acc[0, slot] += dot_nn(activated, down_ref[index, 0])
        acc[1, slot] += dot_nt(pre_grad, up_ref[index, 0])
        for which, grad in enumerate(
            (dot_tn(cand[0, slot], pre_grad), dot_tn(activated, cand[1, slot]))
        ):
            square[which] = grad
            for half in range(halves):
                own = pl.multiple_of((2 * half + parity) * piece, piece)
                other = pl.multiple_of((2 * half + 1 - parity) * piece, piece)
                keep_ref[0, half, which, index] = square[which, pl.ds(own, piece), :]
                send_ref[0, half, which, index] = square[which, pl.ds(other, piece), :]

    @pl.when(step == last)
    def _():
        for copy in acc_copy(True):
            copy.start()
        for bit in range(bits):
            for kind in range(2):
                for row in range(rows):
                    total = acc[kind, local + bit * rows + row]
                    stage[bit, kind, :, pl.ds(row * width, width)] = total.astype(jnp.bfloat16)
            pltpu.make_async_copy(stage.at[bit], sent[bit], out_sems.at[bit]).start()
        for bit in range(bits):
            pltpu.make_async_copy(stage.at[bit], sent[bit], out_sems.at[bit]).wait()
        for copy in acc_copy(True):
            copy.wait()


def main_call(start, rows, slots, parity, inputs, out_grad, arrived, prior, w_up, w_down, halves):
    tokens, features = inputs.shape
    slot_kinds, columns, width, _ = w_up.shape
    local = features // width
    bits = len(arrived)
    cols = columns * rows // local
    slot_count = local + bits * rows
    first = start * columns // local
    has_prior = prior is not None
    piece = width // (2 * halves)
    dims = (local, bits, rows, width, slot_count, halves, first, has_prior)
    anywhere = pl.BlockSpec(memory_space=pl.ANY)
    weight = pl.BlockSpec((slot_kinds, 1, width, width), lambda i, *_: (0, first + i, 0, 0))
    grad_block = pl.BlockSpec((1, halves, 2, slot_kinds, piece, width), lambda i, *_: (i, 0, 0, 0, 0, 0))
    grad_shape = jax.ShapeDtypeStruct((cols, halves, 2, slot_kinds, piece, width), jnp.float32)
    operands = [inputs, out_grad, *arrived] + ([prior] if has_prior else []) + [w_up, w_down]
    pair_flops = 2 * tokens * width * width * 6
    moved = 2 * cols * slot_kinds * width * width * 6 + 12 * tokens * width * slot_count
    return pl.pallas_call(
        functools.partial(main_body, dims),
        grid_spec=pltpu.PrefetchScalarGridSpec(
            num_scalar_prefetch=2,
            grid=(cols,),
            in_specs=[anywhere] * (len(operands) - 2) + [weight, weight],
            out_specs=[anywhere] * (1 + bits) + [grad_block, grad_block],
            scratch_shapes=[
                pltpu.VMEM((2, slot_count, tokens, width), jnp.bfloat16),
                pltpu.VMEM((2, slot_count, tokens, width), jnp.float32),
                pltpu.VMEM((bits, 2, tokens, rows * width), jnp.bfloat16),
                pltpu.VMEM((2, width, width), jnp.float32),
                pltpu.SemaphoreType.DMA((2 * slot_count,)),
                pltpu.SemaphoreType.DMA((2 * local,)),
                pltpu.SemaphoreType.DMA((bits,)),
            ],
        ),
        out_shape=[
            jax.ShapeDtypeStruct((2, local, tokens, width), jnp.float32),
            *[jax.ShapeDtypeStruct((2, tokens, rows * width), jnp.bfloat16)] * bits,
            grad_shape,
            grad_shape,
        ],
        cost_estimate=pl.CostEstimate(
            flops=pair_flops * cols * slot_kinds,
            bytes_accessed=moved,
            transcendentals=2 * cols * tokens * width,
        ),
        compiler_params=pltpu.CompilerParams(
            dimension_semantics=("arbitrary",), vmem_limit_bytes=60 << 20
        ),
        name="columns",
    )(slots, parity, *operands)


def halve_body(parity_ref, keep_ref, recv_ref, kept_ref, send_ref):
    parity = parity_ref[0]
    for half in range(kept_ref.shape[1]):
        own = 2 * half + parity
        other = 2 * half + 1 - parity
        kept_ref[:, half] = keep_ref[:, own] + recv_ref[:, own]
        send_ref[:, half] = keep_ref[:, other] + recv_ref[:, other]


def halve_call(parity, keep, recv):
    cols, halves, pair, slot_kinds, piece, width = keep.shape
    block = min(4, cols)
    spec = pl.BlockSpec((block, halves, pair, slot_kinds, piece, width), lambda i, *_: (i, 0, 0, 0, 0, 0))
    half_shape = (cols, halves // 2, pair, slot_kinds, piece, width)
    half_spec = pl.BlockSpec((block,) + half_shape[1:], lambda i, *_: (i, 0, 0, 0, 0, 0))
    return pl.pallas_call(
        halve_body,
        grid_spec=pltpu.PrefetchScalarGridSpec(
            num_scalar_prefetch=1,
            grid=(cols // block,),
            in_specs=[spec, spec],
            out_specs=[half_spec, half_spec],
        ),
        out_shape=[jax.ShapeDtypeStruct(half_shape, jnp.float32)] * 2,
        cost_estimate=pl.CostEstimate(flops=keep.size, bytes_accessed=12 * keep.size, transcendentals=0),
        name="halve",
    )(parity, keep, recv)


def grads_body(keep_ref, recv_ref, *refs):
    up_ref, down_ref = refs[-2], refs[-1]
    for which, ref in enumerate((up_ref, down_ref)):
        for slot in range(ref.shape[0]):
            ref[slot] = keep_ref[:, 0, which, slot] + recv_ref[:, 0, which, slot]


def grads_call(start, columns, keep, recv, prior):
    cols, _, pair, slot_kinds, piece, width = keep.shape
    block = min(4, cols)
    first = start // block
    spec = pl.BlockSpec((block, 1, pair, slot_kinds, piece, width), lambda i: (i, 0, 0, 0, 0, 0))
    out_spec = pl.BlockSpec((slot_kinds, block, piece, width), lambda i: (0, first + i, 0, 0))
    out_shape = jax.ShapeDtypeStruct((slot_kinds, columns, piece, width), jnp.float32)
    return pl.pallas_call(
        grads_body,
        grid=(cols // block,),
        in_specs=[spec, spec] + [pl.BlockSpec(memory_space=pl.ANY)] * len(prior),
        out_specs=[out_spec, out_spec],
        out_shape=[out_shape, out_shape],
        input_output_aliases={2 + i: i for i in range(len(prior))},
        cost_estimate=pl.CostEstimate(flops=keep.size, bytes_accessed=12 * keep.size, transcendentals=0),
        name="grads",
    )(keep, recv, *prior)


def total_body(bits, acc_ref, *refs):
    out_refs = refs[-2:]
    for kind in range(2):
        total = acc_ref[kind, 0]
        for bit in range(bits):
            total = total + refs[bit][kind].astype(jnp.float32)
        out_refs[kind][...] = total.astype(jnp.bfloat16)


def total_call(start, rows, acc, arrived, prior):
    _, local, tokens, width = acc.shape
    bits = len(arrived)
    tile = tokens // 2
    acc_spec = pl.BlockSpec((2, 1, tile, width), lambda i, t: (0, start + i, t, 0))
    recv_spec = pl.BlockSpec((2, tile, width), lambda i, t: (0, t, i))
    out_spec = pl.BlockSpec((tile, width), lambda i, t: (t, start + i))
    out_shape = jax.ShapeDtypeStruct((tokens, local * width), jnp.bfloat16)
    size = 2 * rows * tokens * width
    return pl.pallas_call(
        functools.partial(total_body, bits),
        grid=(rows, 2),
        in_specs=[acc_spec] + [recv_spec] * bits + [pl.BlockSpec(memory_space=pl.ANY)] * len(prior),
        out_specs=[out_spec, out_spec],
        out_shape=[out_shape, out_shape],
        input_output_aliases={1 + bits + i: i for i in range(len(prior))},
        cost_estimate=pl.CostEstimate(flops=size * bits, bytes_accessed=(6 + 2 * bits) * size, transcendentals=0),
        name="totals",
    )(acc, *arrived, *prior)


def shards(inputs, out_grad, w_up, w_down, partners):
    _, features = inputs.shape
    _, columns, width, _ = w_up.shape
    local = features // width
    bits = lax.axis_size("mp").bit_length() - 1
    dp_bits = lax.axis_size("dp").bit_length() - 1
    sizes = row_groups(local)
    starts = [sum(sizes[:group]) for group in range(len(sizes))]
    per_row = columns // local
    device = lax.axis_index("mp")
    dp_index = lax.axis_index("dp")

    distance = jnp.bitwise_xor(partners // local, device)
    within = partners % local
    level = jnp.zeros_like(distance)
    for bit in range(1, bits):
        level = level + (distance >= 1 << bit).astype(jnp.int32)
    is_local = distance == 0
    parities = [(dp_index // 2**bit % 2).reshape(1).astype(jnp.int32) for bit in range(dp_bits)]

    arrived = []
    for start, rows in zip(starts, sizes):
        pair = pack_call(start, rows, width, inputs, out_grad)
        arrived.append([partner(pair, "mp", bit) for bit in range(bits)])

    acc = None
    returned = []
    kept = []
    for group, (start, rows) in enumerate(zip(starts, sizes)):
        slot = jnp.where(is_local, within, local + level * rows + within - start)
        slots = slot[:, start * per_row : (start + rows) * per_row].reshape(-1)
        acc, *rest = main_call(
            start, rows, slots, parities[0], inputs, out_grad, arrived[group], acc, w_up, w_down,
            2 ** (dp_bits - 1),
        )
        returned.append([partner(rest[bit], "mp", bit) for bit in range(bits)])
        keep, send = rest[bits:]
        for bit in range(1, dp_bits):
            recv = partner(send, "dp", bit - 1)
            keep, send = halve_call(parities[bit], keep, recv)
        kept.append((keep, partner(send, "dp", dp_bits - 1)))

    grads = []
    for group, start in enumerate(starts):
        grads = grads_call(start * per_row, columns, *kept[group], grads)
    totals = []
    for group, (start, rows) in enumerate(zip(starts, sizes)):
        totals = total_call(start, rows, acc, returned[group], totals)
    return (*totals, *grads)


def solution(mesh):
    in_specs = (
        P("dp", "mp"),
        P("dp", "mp"),
        P(None, "mp", None, None),
        P(None, "mp", None, None),
        P(None, "mp"),
    )
    out_specs = (P("dp", "mp"), P("dp", "mp"), P(None, "mp", "dp", None), P(None, "mp", "dp", None))

    return jax.shard_map(shards, mesh=mesh, in_specs=in_specs, out_specs=out_specs, check_vma=False)
```

```python
import functools

import jax
import jax.numpy as jnp
from jax import lax
from jax.experimental import pallas as pl
from jax.experimental.pallas import tpu as pltpu
from jax.sharding import PartitionSpec as P


def row_groups(local):
    edge = max(1, local // 8)
    middle = local - 2 * edge
    sizes = [edge, middle - middle // 2, middle // 2, edge] if middle >= 0 else [local]
    return [size for size in sizes if size > 0]


def partner(value, axis, distance):
    mask = 2**distance
    pairs = [(source, source ^ mask) for source in range(lax.axis_size(axis))]
    return lax.ppermute(value, axis, pairs)


def gelu_pair(hidden):
    erf_part = lax.erf(hidden * 0.7071067811865476)
    value = 0.5 * hidden * (1.0 + erf_part)
    slope = 0.5 * (1.0 + erf_part) + hidden * jnp.exp(-0.5 * hidden * hidden) * 0.3989422804014327
    return value, slope


def dot_nn(left, right):
    return lax.dot_general(left, right, (((1,), (0,)), ((), ())), preferred_element_type=jnp.float32)


def dot_nt(left, right):
    return lax.dot_general(left, right, (((1,), (1,)), ((), ())), preferred_element_type=jnp.float32)


def dot_tn(left, right):
    return lax.dot_general(left, right, (((0,), (0,)), ((), ())), preferred_element_type=jnp.float32)


def pack_body(x_ref, g_ref, pair_ref):
    pair_ref[0] = x_ref[...]
    pair_ref[1] = g_ref[...]


def pack_call(start, rows, width, inputs, out_grad):
    tokens = inputs.shape[0]
    column = pl.BlockSpec((tokens, width), lambda i: (0, start + i))
    size = 2 * tokens * rows * width
    return pl.pallas_call(
        pack_body,
        grid=(rows,),
        in_specs=[column, column],
        out_specs=pl.BlockSpec((2, tokens, width), lambda i: (0, 0, i)),
        out_shape=jax.ShapeDtypeStruct((2, tokens, rows * width), inputs.dtype),
        cost_estimate=pl.CostEstimate(flops=0, bytes_accessed=4 * size, transcendentals=0),
        name="pack",
    )(inputs, out_grad)


def main_body(dims, slots_ref, parity_ref, *refs):
    local, bits, rows, width, _, halves, _, has_prior = dims
    x_hbm, g_hbm = refs[0], refs[1]
    arrived = refs[2 : 2 + bits]
    at = 2 + bits
    prior = refs[at] if has_prior else None
    at += int(has_prior)
    up_ref, down_ref = refs[at], refs[at + 1]
    acc_hbm = refs[at + 2]
    sent = refs[at + 3 : at + 3 + bits]
    keep_ref, send_ref = refs[at + 3 + bits], refs[at + 4 + bits]
    cand, acc, stage, square, in_sems, acc_sems, out_sems = refs[at + 5 + bits :]
    step = pl.program_id(0)
    last = pl.num_programs(0) - 1

    def loads():
        copies = []
        for kind, source in enumerate((x_hbm, g_hbm)):
            for block in range(local):
                view = source.at[:, pl.ds(block * width, width)]
                copies.append((view, cand.at[kind, block]))
        for kind in range(2):
            for bit in range(bits):
                for row in range(rows):
                    view = arrived[bit].at[kind, :, pl.ds(row * width, width)]
                    copies.append((view, cand.at[kind, local + bit * rows + row]))
        return [pltpu.make_async_copy(a, b, in_sems.at[i]) for i, (a, b) in enumerate(copies)]

    def acc_copy(store):
        copies = []
        for kind in range(2):
            for block in range(local):
                index = kind * local + block
                far = acc_hbm if store else prior
                ends = (acc.at[kind, block], far.at[kind, block])
                ends = ends if store else ends[::-1]
                copies.append(pltpu.make_async_copy(*ends, acc_sems.at[index]))
        return copies

    @pl.when(step == 0)
    def _():
        for copy in loads():
            copy.start()
        if has_prior:
            for copy in acc_copy(False):
                copy.start()
        start = local if has_prior else 0
        tokens = acc.shape[2]
        for kind in range(2):

            @pl.loop(start, acc.shape[1])
            def _(slot):
                acc[kind, slot] = jnp.zeros((tokens, width), jnp.float32)

        if has_prior:
            for copy in acc_copy(False):
                copy.wait()
        for copy in loads():
            copy.wait()

    first_slot = slots_ref[step]
    second_slot = slots_ref[pl.num_programs(0) + step]
    slots = (first_slot, second_slot)
    pre_act = dot_nn(cand[0, first_slot], up_ref[0, 0]) + dot_nn(cand[0, second_slot], up_ref[1, 0])
    value, slope = gelu_pair(pre_act)
    activated = value.astype(jnp.bfloat16)
    hidden_grad = dot_nt(cand[1, first_slot], down_ref[0, 0])
    hidden_grad = hidden_grad + dot_nt(cand[1, second_slot], down_ref[1, 0])
    pre_grad = (hidden_grad * slope).astype(jnp.bfloat16)
    parity = parity_ref[0]
    piece = width // (2 * halves)
    for index, slot in enumerate(slots):
        acc[0, slot] += dot_nn(activated, down_ref[index, 0])
        acc[1, slot] += dot_nt(pre_grad, up_ref[index, 0])
        for which, grad in enumerate(
            (dot_tn(cand[0, slot], pre_grad), dot_tn(activated, cand[1, slot]))
        ):
            square[which] = grad
            for half in range(halves):
                own = pl.multiple_of((2 * half + parity) * piece, piece)
                other = pl.multiple_of((2 * half + 1 - parity) * piece, piece)
                keep_ref[0, half, which, index] = square[which, pl.ds(own, piece), :]
                send_ref[0, half, which, index] = square[which, pl.ds(other, piece), :]

    @pl.when(step == last)
    def _():
        for copy in acc_copy(True):
            copy.start()
        for bit in range(bits):
            for kind in range(2):
                for row in range(rows):
                    total = acc[kind, local + bit * rows + row]
                    stage[bit, kind, :, pl.ds(row * width, width)] = total.astype(jnp.bfloat16)
            pltpu.make_async_copy(stage.at[bit], sent[bit], out_sems.at[bit]).start()
        for bit in range(bits):
            pltpu.make_async_copy(stage.at[bit], sent[bit], out_sems.at[bit]).wait()
        for copy in acc_copy(True):
            copy.wait()


def main_call(start, rows, slots, parity, inputs, out_grad, arrived, prior, w_up, w_down, halves):
    tokens, features = inputs.shape
    slot_kinds, columns, width, _ = w_up.shape
    local = features // width
    bits = len(arrived)
    cols = columns * rows // local
    slot_count = local + bits * rows
    first = start * columns // local
    has_prior = prior is not None
    piece = width // (2 * halves)
    dims = (local, bits, rows, width, slot_count, halves, first, has_prior)
    anywhere = pl.BlockSpec(memory_space=pl.ANY)
    weight = pl.BlockSpec((slot_kinds, 1, width, width), lambda i, *_: (0, first + i, 0, 0))
    grad_block = pl.BlockSpec((1, halves, 2, slot_kinds, piece, width), lambda i, *_: (i, 0, 0, 0, 0, 0))
    grad_shape = jax.ShapeDtypeStruct((cols, halves, 2, slot_kinds, piece, width), jnp.float32)
    operands = [inputs, out_grad, *arrived] + ([prior] if has_prior else []) + [w_up, w_down]
    pair_flops = 2 * tokens * width * width * 6
    moved = 2 * cols * slot_kinds * width * width * 6 + 12 * tokens * width * slot_count
    return pl.pallas_call(
        functools.partial(main_body, dims),
        grid_spec=pltpu.PrefetchScalarGridSpec(
            num_scalar_prefetch=2,
            grid=(cols,),
            in_specs=[anywhere] * (len(operands) - 2) + [weight, weight],
            out_specs=[anywhere] * (1 + bits) + [grad_block, grad_block],
            scratch_shapes=[
                pltpu.VMEM((2, slot_count, tokens, width), jnp.bfloat16),
                pltpu.VMEM((2, slot_count, tokens, width), jnp.float32),
                pltpu.VMEM((bits, 2, tokens, rows * width), jnp.bfloat16),
                pltpu.VMEM((2, width, width), jnp.float32),
                pltpu.SemaphoreType.DMA((2 * slot_count,)),
                pltpu.SemaphoreType.DMA((2 * local,)),
                pltpu.SemaphoreType.DMA((bits,)),
            ],
        ),
        out_shape=[
            jax.ShapeDtypeStruct((2, local, tokens, width), jnp.float32),
            *[jax.ShapeDtypeStruct((2, tokens, rows * width), jnp.bfloat16)] * bits,
            grad_shape,
            grad_shape,
        ],
        cost_estimate=pl.CostEstimate(
            flops=pair_flops * cols * slot_kinds,
            bytes_accessed=moved,
            transcendentals=2 * cols * tokens * width,
        ),
        compiler_params=pltpu.CompilerParams(
            dimension_semantics=("arbitrary",), vmem_limit_bytes=60 << 20
        ),
        name="columns",
    )(slots, parity, *operands)


def halve_body(parity_ref, keep_ref, recv_ref, kept_ref, send_ref):
    parity = parity_ref[0]
    for half in range(kept_ref.shape[1]):
        own = 2 * half + parity
        other = 2 * half + 1 - parity
        kept_ref[:, half] = keep_ref[:, own] + recv_ref[:, own]
        send_ref[:, half] = keep_ref[:, other] + recv_ref[:, other]


def halve_call(per_row, parity, keep, recv):
    cols, halves, pair, slot_kinds, piece, width = keep.shape
    block = per_row
    spec = pl.BlockSpec((block, halves, pair, slot_kinds, piece, width), lambda i, *_: (i, 0, 0, 0, 0, 0))
    half_shape = (cols, halves // 2, pair, slot_kinds, piece, width)
    half_spec = pl.BlockSpec((block,) + half_shape[1:], lambda i, *_: (i, 0, 0, 0, 0, 0))
    return pl.pallas_call(
        halve_body,
        grid_spec=pltpu.PrefetchScalarGridSpec(
            num_scalar_prefetch=1,
            grid=(cols // block,),
            in_specs=[spec, spec],
            out_specs=[half_spec, half_spec],
        ),
        out_shape=[jax.ShapeDtypeStruct(half_shape, jnp.float32)] * 2,
        cost_estimate=pl.CostEstimate(flops=keep.size, bytes_accessed=12 * keep.size, transcendentals=0),
        name="halve",
    )(parity, keep, recv)


def grads_body(keep_ref, recv_ref, *refs):
    up_ref, down_ref = refs[-2], refs[-1]
    for which, ref in enumerate((up_ref, down_ref)):
        for slot in range(ref.shape[0]):
            ref[slot] = keep_ref[:, 0, which, slot] + recv_ref[:, 0, which, slot]


def grads_call(start, per_row, columns, keep, recv, prior):
    cols, _, pair, slot_kinds, piece, width = keep.shape
    block = per_row
    first = start
    spec = pl.BlockSpec((block, 1, pair, slot_kinds, piece, width), lambda i: (i, 0, 0, 0, 0, 0))
    out_spec = pl.BlockSpec((slot_kinds, block, piece, width), lambda i: (0, first + i, 0, 0))
    out_shape = jax.ShapeDtypeStruct((slot_kinds, columns, piece, width), jnp.float32)
    return pl.pallas_call(
        grads_body,
        grid=(cols // block,),
        in_specs=[spec, spec] + [pl.BlockSpec(memory_space=pl.ANY)] * len(prior),
        out_specs=[out_spec, out_spec],
        out_shape=[out_shape, out_shape],
        input_output_aliases={2 + i: i for i in range(len(prior))},
        cost_estimate=pl.CostEstimate(flops=keep.size, bytes_accessed=12 * keep.size, transcendentals=0),
        name="grads",
    )(keep, recv, *prior)


def total_body(bits, acc_ref, *refs):
    out_refs = refs[-2:]
    for kind in range(2):
        total = acc_ref[kind, 0]
        for bit in range(bits):
            total = total + refs[bit][kind].astype(jnp.float32)
        out_refs[kind][...] = total.astype(jnp.bfloat16)


def total_call(start, rows, acc, arrived, prior):
    _, local, tokens, width = acc.shape
    bits = len(arrived)
    tile = tokens // 2
    acc_spec = pl.BlockSpec((2, 1, tile, width), lambda i, t: (0, start + i, t, 0))
    recv_spec = pl.BlockSpec((2, tile, width), lambda i, t: (0, t, i))
    out_spec = pl.BlockSpec((tile, width), lambda i, t: (t, start + i))
    out_shape = jax.ShapeDtypeStruct((tokens, local * width), jnp.bfloat16)
    size = 2 * rows * tokens * width
    return pl.pallas_call(
        functools.partial(total_body, bits),
        grid=(rows, 2),
        in_specs=[acc_spec] + [recv_spec] * bits + [pl.BlockSpec(memory_space=pl.ANY)] * len(prior),
        out_specs=[out_spec, out_spec],
        out_shape=[out_shape, out_shape],
        input_output_aliases={1 + bits + i: i for i in range(len(prior))},
        cost_estimate=pl.CostEstimate(flops=size * bits, bytes_accessed=(6 + 2 * bits) * size, transcendentals=0),
        name="totals",
    )(acc, *arrived, *prior)


def shards(inputs, out_grad, w_up, w_down, partners):
    _, features = inputs.shape
    _, columns, width, _ = w_up.shape
    local = features // width
    bits = lax.axis_size("mp").bit_length() - 1
    dp_bits = lax.axis_size("dp").bit_length() - 1
    sizes = row_groups(local)
    starts = [sum(sizes[:group]) for group in range(len(sizes))]
    per_row = columns // local
    device = lax.axis_index("mp")
    dp_index = lax.axis_index("dp")

    distance = jnp.bitwise_xor(partners // local, device)
    within = partners % local
    level = jnp.zeros_like(distance)
    for bit in range(1, bits):
        level = level + (distance >= 1 << bit).astype(jnp.int32)
    is_local = distance == 0
    parities = [(dp_index // 2**bit % 2).reshape(1).astype(jnp.int32) for bit in range(dp_bits)]

    arrived = []
    for start, rows in zip(starts, sizes):
        pair = pack_call(start, rows, width, inputs, out_grad)
        arrived.append([partner(pair, "mp", bit) for bit in range(bits)])

    acc = None
    returned = []
    kept = []
    for group, (start, rows) in enumerate(zip(starts, sizes)):
        slot = jnp.where(is_local, within, local + level * rows + within - start)
        slots = slot[:, start * per_row : (start + rows) * per_row].reshape(-1)
        acc, *rest = main_call(
            start, rows, slots, parities[0], inputs, out_grad, arrived[group], acc, w_up, w_down,
            2 ** (dp_bits - 1),
        )
        returned.append([partner(rest[bit], "mp", bit) for bit in range(bits)])
        keep, send = rest[bits:]
        for bit in range(1, dp_bits):
            recv = partner(send, "dp", bit - 1)
            keep, send = halve_call(per_row, parities[bit], keep, recv)
        kept.append((keep, partner(send, "dp", dp_bits - 1)))

    grads = []
    for group, start in enumerate(starts):
        grads = grads_call(start, per_row, columns, *kept[group], grads)
    totals = []
    for group, (start, rows) in enumerate(zip(starts, sizes)):
        totals = total_call(start, rows, acc, returned[group], totals)
    return (*totals, *grads)


def solution(mesh):
    in_specs = (
        P("dp", "mp"),
        P("dp", "mp"),
        P(None, "mp", None, None),
        P(None, "mp", None, None),
        P(None, "mp"),
    )
    out_specs = (P("dp", "mp"), P("dp", "mp"), P(None, "mp", "dp", None), P(None, "mp", "dp", None))

    return jax.shard_map(shards, mesh=mesh, in_specs=in_specs, out_specs=out_specs, check_vma=False)
```

```python
import functools

import jax
import jax.numpy as jnp
from jax import lax
from jax.experimental import pallas as pl
from jax.experimental.pallas import tpu as pltpu
from jax.sharding import PartitionSpec as P


def row_groups(local):
    edge = max(1, local // 8)
    middle = local - 2 * edge
    sizes = [edge, middle - middle // 2, middle // 2, edge] if middle >= 0 else [local]
    return [size for size in sizes if size > 0]


def partner(value, axis, distance):
    mask = 2**distance
    pairs = [(source, source ^ mask) for source in range(lax.axis_size(axis))]
    return lax.ppermute(value, axis, pairs)


def gelu_pair(hidden):
    erf_part = lax.erf(hidden * 0.7071067811865476)
    value = 0.5 * hidden * (1.0 + erf_part)
    slope = 0.5 * (1.0 + erf_part) + hidden * jnp.exp(-0.5 * hidden * hidden) * 0.3989422804014327
    return value, slope


def dot_nn(left, right):
    return lax.dot_general(left, right, (((1,), (0,)), ((), ())), preferred_element_type=jnp.float32)


def dot_nt(left, right):
    return lax.dot_general(left, right, (((1,), (1,)), ((), ())), preferred_element_type=jnp.float32)


def dot_tn(left, right):
    return lax.dot_general(left, right, (((0,), (0,)), ((), ())), preferred_element_type=jnp.float32)


def pack_body(*refs):
    pair_ref = refs[-1]
    for kind, ref in enumerate(refs[:-1]):
        pair_ref[kind] = ref[...]


def pack_call(start, rows, width, *arrays):
    tokens = arrays[0].shape[0]
    kinds = len(arrays)
    column = pl.BlockSpec((tokens, width), lambda i: (0, start + i))
    size = kinds * tokens * rows * width
    return pl.pallas_call(
        pack_body,
        grid=(rows,),
        in_specs=[column] * kinds,
        out_specs=pl.BlockSpec((kinds, tokens, width), lambda i: (0, 0, i)),
        out_shape=jax.ShapeDtypeStruct((kinds, tokens, rows * width), arrays[0].dtype),
        cost_estimate=pl.CostEstimate(flops=0, bytes_accessed=4 * size, transcendentals=0),
        name="pack",
    )(*arrays)


def main_body(dims, slots_ref, parity_ref, *refs):
    local, bits, rows, width, _, halves, _, has_prior, apart, came_apart = dims
    x_hbm, g_hbm = refs[0], refs[1]
    arrived = refs[2 : 2 + bits * (1 + int(came_apart))]
    at = 2 + len(arrived)
    prior = refs[at] if has_prior else None
    at += int(has_prior)
    up_ref, down_ref = refs[at], refs[at + 1]
    acc_hbm = refs[at + 2]
    outs = refs[at + 3 : at + 3 + bits * (1 + int(apart))]
    at += 3 + len(outs)
    keep_ref, send_ref = refs[at], refs[at + 1]
    cand, acc, stage, square, in_sems, acc_sems, out_sems = refs[at + 2 :]
    step = pl.program_id(0)
    last = pl.num_programs(0) - 1

    def loads():
        copies = []
        for kind, source in enumerate((x_hbm, g_hbm)):
            for block in range(local):
                view = source.at[:, pl.ds(block * width, width)]
                copies.append((view, cand.at[kind, block]))
        for kind in range(2):
            for bit in range(bits):
                for row in range(rows):
                    whole = arrived[2 * bit + kind].at[0] if came_apart else arrived[bit].at[kind]
                    view = whole.at[:, pl.ds(row * width, width)]
                    copies.append((view, cand.at[kind, local + bit * rows + row]))
        return [pltpu.make_async_copy(a, b, in_sems.at[i]) for i, (a, b) in enumerate(copies)]

    def acc_copy(store):
        copies = []
        for kind in range(2):
            for block in range(local):
                index = kind * local + block
                far = acc_hbm if store else prior
                ends = (acc.at[kind, block], far.at[kind, block])
                ends = ends if store else ends[::-1]
                copies.append(pltpu.make_async_copy(*ends, acc_sems.at[index]))
        return copies

    def out_copy(bit, kind):
        far = outs[2 * bit + kind].at[0] if apart else outs[bit].at[kind]
        return pltpu.make_async_copy(stage.at[bit, kind], far, out_sems.at[2 * bit + kind])

    @pl.when(step == 0)
    def _():
        for copy in loads():
            copy.start()
        if has_prior:
            for copy in acc_copy(False):
                copy.start()
        start = local if has_prior else 0
        tokens = acc.shape[2]
        for kind in range(2):

            @pl.loop(start, acc.shape[1])
            def _(slot):
                acc[kind, slot] = jnp.zeros((tokens, width), jnp.float32)

        if has_prior:
            for copy in acc_copy(False):
                copy.wait()
        for copy in loads():
            copy.wait()

    first_slot = slots_ref[step]
    second_slot = slots_ref[pl.num_programs(0) + step]
    slots = (first_slot, second_slot)
    pre_act = dot_nn(cand[0, first_slot], up_ref[0, 0]) + dot_nn(cand[0, second_slot], up_ref[1, 0])
    value, slope = gelu_pair(pre_act)
    activated = value.astype(jnp.bfloat16)
    hidden_grad = dot_nt(cand[1, first_slot], down_ref[0, 0])
    hidden_grad = hidden_grad + dot_nt(cand[1, second_slot], down_ref[1, 0])
    pre_grad = (hidden_grad * slope).astype(jnp.bfloat16)
    parity = parity_ref[0]
    piece = width // (2 * halves)
    for index, slot in enumerate(slots):
        acc[0, slot] += dot_nn(activated, down_ref[index, 0])
        acc[1, slot] += dot_nt(pre_grad, up_ref[index, 0])
        for which, grad in enumerate(
            (dot_tn(cand[0, slot], pre_grad), dot_tn(activated, cand[1, slot]))
        ):
            square[which] = grad
            for half in range(halves):
                own = pl.multiple_of((2 * half + parity) * piece, piece)
                other = pl.multiple_of((2 * half + 1 - parity) * piece, piece)
                keep_ref[0, half, which, index] = square[which, pl.ds(own, piece), :]
                send_ref[0, half, which, index] = square[which, pl.ds(other, piece), :]

    @pl.when(step == last)
    def _():
        for copy in acc_copy(True):
            copy.start()
        order = [(bit, kind) for bit in range(bits) for kind in range(2)]
        for bit, kind in order:
            for row in range(rows):
                total = acc[kind, local + bit * rows + row]
                stage[bit, kind, :, pl.ds(row * width, width)] = total.astype(jnp.bfloat16)
            out_copy(bit, kind).start()
        for bit, kind in order:
            out_copy(bit, kind).wait()
        for copy in acc_copy(True):
            copy.wait()


def main_call(start, rows, slots, parity, inputs, out_grad, arrived, prior, w_up, w_down, halves, apart):
    tokens, features = inputs.shape
    slot_kinds, columns, width, _ = w_up.shape
    local = features // width
    came_apart = arrived[0].shape[0] == 1
    bits = len(arrived) // (1 + int(came_apart))
    cols = columns * rows // local
    slot_count = local + bits * rows
    first = start * columns // local
    has_prior = prior is not None
    piece = width // (2 * halves)
    dims = (local, bits, rows, width, slot_count, halves, first, has_prior, apart, came_apart)
    sends = bits * (1 + int(apart))
    anywhere = pl.BlockSpec(memory_space=pl.ANY)
    weight = pl.BlockSpec((slot_kinds, 1, width, width), lambda i, *_: (0, first + i, 0, 0))
    grad_block = pl.BlockSpec((1, halves, 2, slot_kinds, piece, width), lambda i, *_: (i, 0, 0, 0, 0, 0))
    grad_shape = jax.ShapeDtypeStruct((cols, halves, 2, slot_kinds, piece, width), jnp.float32)
    operands = [inputs, out_grad, *arrived] + ([prior] if has_prior else []) + [w_up, w_down]
    pair_flops = 2 * tokens * width * width * 6
    moved = 2 * cols * slot_kinds * width * width * 6 + 12 * tokens * width * slot_count
    return pl.pallas_call(
        functools.partial(main_body, dims),
        grid_spec=pltpu.PrefetchScalarGridSpec(
            num_scalar_prefetch=2,
            grid=(cols,),
            in_specs=[anywhere] * (len(operands) - 2) + [weight, weight],
            out_specs=[anywhere] * (1 + sends) + [grad_block, grad_block],
            scratch_shapes=[
                pltpu.VMEM((2, slot_count, tokens, width), jnp.bfloat16),
                pltpu.VMEM((2, slot_count, tokens, width), jnp.float32),
                pltpu.VMEM((bits, 2, tokens, rows * width), jnp.bfloat16),
                pltpu.VMEM((2, width, width), jnp.float32),
                pltpu.SemaphoreType.DMA((2 * slot_count,)),
                pltpu.SemaphoreType.DMA((2 * local,)),
                pltpu.SemaphoreType.DMA((2 * bits,)),
            ],
        ),
        out_shape=[
            jax.ShapeDtypeStruct((2, local, tokens, width), jnp.float32),
            *[jax.ShapeDtypeStruct((2 * bits // sends, tokens, rows * width), jnp.bfloat16)] * sends,
            grad_shape,
            grad_shape,
        ],
        cost_estimate=pl.CostEstimate(
            flops=pair_flops * cols * slot_kinds,
            bytes_accessed=moved,
            transcendentals=2 * cols * tokens * width,
        ),
        compiler_params=pltpu.CompilerParams(
            dimension_semantics=("arbitrary",), vmem_limit_bytes=60 << 20
        ),
        name="columns",
    )(slots, parity, *operands)


def halve_body(parity_ref, keep_ref, recv_ref, kept_ref, send_ref):
    parity = parity_ref[0]
    for half in range(kept_ref.shape[1]):
        own = 2 * half + parity
        other = 2 * half + 1 - parity
        kept_ref[:, half] = keep_ref[:, own] + recv_ref[:, own]
        send_ref[:, half] = keep_ref[:, other] + recv_ref[:, other]


def halve_call(per_row, parity, keep, recv):
    cols, halves, pair, slot_kinds, piece, width = keep.shape
    block = per_row
    spec = pl.BlockSpec((block, halves, pair, slot_kinds, piece, width), lambda i, *_: (i, 0, 0, 0, 0, 0))
    half_shape = (cols, halves // 2, pair, slot_kinds, piece, width)
    half_spec = pl.BlockSpec((block,) + half_shape[1:], lambda i, *_: (i, 0, 0, 0, 0, 0))
    return pl.pallas_call(
        halve_body,
        grid_spec=pltpu.PrefetchScalarGridSpec(
            num_scalar_prefetch=1,
            grid=(cols // block,),
            in_specs=[spec, spec],
            out_specs=[half_spec, half_spec],
        ),
        out_shape=[jax.ShapeDtypeStruct(half_shape, jnp.float32)] * 2,
        cost_estimate=pl.CostEstimate(flops=keep.size, bytes_accessed=12 * keep.size, transcendentals=0),
        name="halve",
    )(parity, keep, recv)


def grads_body(keep_ref, recv_ref, *refs):
    up_ref, down_ref = refs[-2], refs[-1]
    for which, ref in enumerate((up_ref, down_ref)):
        for slot in range(ref.shape[0]):
            ref[slot] = keep_ref[:, 0, which, slot] + recv_ref[:, 0, which, slot]


def grads_call(start, per_row, columns, keep, recv, prior):
    cols, _, pair, slot_kinds, piece, width = keep.shape
    block = per_row
    first = start
    spec = pl.BlockSpec((block, 1, pair, slot_kinds, piece, width), lambda i: (i, 0, 0, 0, 0, 0))
    out_spec = pl.BlockSpec((slot_kinds, block, piece, width), lambda i: (0, first + i, 0, 0))
    out_shape = jax.ShapeDtypeStruct((slot_kinds, columns, piece, width), jnp.float32)
    return pl.pallas_call(
        grads_body,
        grid=(cols // block,),
        in_specs=[spec, spec] + [pl.BlockSpec(memory_space=pl.ANY)] * len(prior),
        out_specs=[out_spec, out_spec],
        out_shape=[out_shape, out_shape],
        input_output_aliases={2 + i: i for i in range(len(prior))},
        cost_estimate=pl.CostEstimate(flops=keep.size, bytes_accessed=12 * keep.size, transcendentals=0),
        name="grads",
    )(keep, recv, *prior)


def total_body(bits, kinds, acc_ref, *refs):
    out_refs = refs[-kinds:]
    for kind in range(kinds):
        total = acc_ref[kind, 0]
        for bit in range(bits):
            total = total + refs[bit][kind].astype(jnp.float32)
        out_refs[kind][...] = total.astype(jnp.bfloat16)


def total_call(start, rows, first_kind, acc, arrived, prior):
    _, local, tokens, width = acc.shape
    bits = len(arrived)
    kinds = arrived[0].shape[0]
    tile = tokens // 2
    acc_spec = pl.BlockSpec((kinds, 1, tile, width), lambda i, t: (first_kind, start + i, t, 0))
    recv_spec = pl.BlockSpec((kinds, tile, width), lambda i, t: (0, t, i))
    out_spec = pl.BlockSpec((tile, width), lambda i, t: (t, start + i))
    out_shape = jax.ShapeDtypeStruct((tokens, local * width), jnp.bfloat16)
    size = kinds * rows * tokens * width
    return pl.pallas_call(
        functools.partial(total_body, bits, kinds),
        grid=(rows, 2),
        in_specs=[acc_spec] + [recv_spec] * bits + [pl.BlockSpec(memory_space=pl.ANY)] * len(prior),
        out_specs=[out_spec] * kinds,
        out_shape=[out_shape] * kinds,
        input_output_aliases={1 + bits + i: i for i in range(len(prior))},
        cost_estimate=pl.CostEstimate(flops=size * bits, bytes_accessed=(6 + 2 * bits) * size, transcendentals=0),
        name="totals",
    )(acc, *arrived, *prior)


def last_total(start, rows, acc, arrived, whole):
    _, _, width = acc.shape
    for row in range(rows):
        lanes = slice(row * width, (row + 1) * width)
        total = acc[start + row]
        for value in arrived:
            total = total + value[0, :, lanes].astype(jnp.float32)
        whole = lax.dynamic_update_slice(whole, total.astype(whole.dtype), (0, (start + row) * width))
    return whole


def shards(inputs, out_grad, w_up, w_down, partners):
    _, features = inputs.shape
    _, columns, width, _ = w_up.shape
    local = features // width
    bits = lax.axis_size("mp").bit_length() - 1
    dp_bits = lax.axis_size("dp").bit_length() - 1
    sizes = row_groups(local)
    starts = [sum(sizes[:group]) for group in range(len(sizes))]
    per_row = columns // local
    last = len(sizes) - 1
    device = lax.axis_index("mp")
    dp_index = lax.axis_index("dp")

    distance = jnp.bitwise_xor(partners // local, device)
    within = partners % local
    level = jnp.zeros_like(distance)
    for bit in range(1, bits):
        level = level + (distance >= 1 << bit).astype(jnp.int32)
    is_local = distance == 0
    parities = [(dp_index // 2**bit % 2).reshape(1).astype(jnp.int32) for bit in range(dp_bits)]

    arrived = []
    for group, (start, rows) in enumerate(zip(starts, sizes)):
        if group == 0:
            parts = []
            for kind, array in enumerate((inputs, out_grad)):
                if kind == 0:
                    block = array[None, :, start * width : (start + rows) * width]
                else:
                    block = pack_call(start, rows, width, array)
                parts.append([partner(block, "mp", bit) for bit in range(bits)])
            arrived.append([parts[kind][bit] for bit in range(bits) for kind in range(2)])
        else:
            pair = pack_call(start, rows, width, inputs, out_grad)
            arrived.append([partner(pair, "mp", bit) for bit in range(bits)])

    acc = None
    returned = []
    kept = []
    for group, (start, rows) in enumerate(zip(starts, sizes)):
        slot = jnp.where(is_local, within, local + level * rows + within - start)
        slots = slot[:, start * per_row : (start + rows) * per_row].reshape(-1)
        acc, *rest = main_call(
            start, rows, slots, parities[0], inputs, out_grad, arrived[group], acc, w_up, w_down,
            2 ** (dp_bits - 1), group == last,
        )
        sends = rest[:-2]
        keep, send = rest[-2:]
        if group == last:
            parts = []
            for kind in range(2):
                parts.append([partner(sends[2 * bit + kind], "mp", bit) for bit in range(bits)])
            returned.append(parts)
        else:
            returned.append([partner(sends[bit], "mp", bit) for bit in range(bits)])
        for bit in range(1, dp_bits):
            recv = partner(send, "dp", bit - 1)
            keep, send = halve_call(per_row, parities[bit], keep, recv)
        kept.append((keep, partner(send, "dp", dp_bits - 1)))

    grads = []
    for group, start in enumerate(starts):
        grads = grads_call(start, per_row, columns, *kept[group], grads)
    totals = []
    for group, (start, rows) in enumerate(zip(starts[:-1], sizes[:-1])):
        totals = total_call(start, rows, 0, acc, returned[group], totals)
    ends = []
    for kind in range(2):
        ends.append(last_total(starts[-1], sizes[-1], acc[kind], returned[-1][kind], totals[kind]))
    return (*ends, *grads)


def solution(mesh):
    in_specs = (
        P("dp", "mp"),
        P("dp", "mp"),
        P(None, "mp", None, None),
        P(None, "mp", None, None),
        P(None, "mp"),
    )
    out_specs = (P("dp", "mp"), P("dp", "mp"), P(None, "mp", "dp", None), P(None, "mp", "dp", None))

    return jax.shard_map(shards, mesh=mesh, in_specs=in_specs, out_specs=out_specs, check_vma=False)
```

```python
import functools

import jax
import jax.numpy as jnp
from jax import lax
from jax.experimental import pallas as pl
from jax.experimental.pallas import tpu as pltpu
from jax.sharding import PartitionSpec as P


def row_groups(local):
    edge = max(1, local // 8)
    middle = local - 2 * edge
    sizes = [edge, middle - middle // 2, middle // 2, edge] if middle >= 0 else [local]
    return [size for size in sizes if size > 0]


def partner(value, axis, distance):
    mask = 2**distance
    pairs = [(source, source ^ mask) for source in range(lax.axis_size(axis))]
    return lax.ppermute(value, axis, pairs)


def gelu_pair(hidden):
    erf_part = lax.erf(hidden * 0.7071067811865476)
    value = 0.5 * hidden * (1.0 + erf_part)
    slope = 0.5 * (1.0 + erf_part) + hidden * jnp.exp(-0.5 * hidden * hidden) * 0.3989422804014327
    return value, slope


def dot_nn(left, right):
    return lax.dot_general(left, right, (((1,), (0,)), ((), ())), preferred_element_type=jnp.float32)


def dot_nt(left, right):
    return lax.dot_general(left, right, (((1,), (1,)), ((), ())), preferred_element_type=jnp.float32)


def dot_tn(left, right):
    return lax.dot_general(left, right, (((0,), (0,)), ((), ())), preferred_element_type=jnp.float32)


def pack_body(*refs):
    pair_ref = refs[-1]
    for kind, ref in enumerate(refs[:-1]):
        pair_ref[kind] = ref[...]


def pack_call(start, rows, width, *arrays):
    tokens = arrays[0].shape[0]
    kinds = len(arrays)
    column = pl.BlockSpec((tokens, width), lambda i: (0, start + i))
    size = kinds * tokens * rows * width
    return pl.pallas_call(
        pack_body,
        grid=(rows,),
        in_specs=[column] * kinds,
        out_specs=pl.BlockSpec((kinds, tokens, width), lambda i: (0, 0, i)),
        out_shape=jax.ShapeDtypeStruct((kinds, tokens, rows * width), arrays[0].dtype),
        cost_estimate=pl.CostEstimate(flops=0, bytes_accessed=4 * size, transcendentals=0),
        name="pack",
    )(*arrays)


def main_body(dims, slots_ref, parity_ref, *refs):
    local, bits, rows, width, _, halves, _, has_prior, apart, came_apart = dims
    x_hbm, g_hbm = refs[0], refs[1]
    arrived = refs[2 : 2 + bits * (1 + int(came_apart))]
    at = 2 + len(arrived)
    prior = refs[at] if has_prior else None
    at += int(has_prior)
    up_ref, down_ref = refs[at], refs[at + 1]
    acc_hbm = refs[at + 2]
    outs = refs[at + 3 : at + 3 + bits * (1 + int(apart))]
    at += 3 + len(outs)
    keep_ref, send_ref = refs[at], refs[at + 1]
    cand, acc, stage, square, in_sems, acc_sems, out_sems = refs[at + 2 :]
    step = pl.program_id(0)
    last = pl.num_programs(0) - 1

    def loads():
        copies = []
        for kind, source in enumerate((x_hbm, g_hbm)):
            for block in range(local):
                view = source.at[:, pl.ds(block * width, width)]
                copies.append((view, cand.at[kind, block]))
        for kind in range(2):
            for bit in range(bits):
                for row in range(rows):
                    whole = arrived[2 * bit + kind].at[0] if came_apart else arrived[bit].at[kind]
                    view = whole.at[:, pl.ds(row * width, width)]
                    copies.append((view, cand.at[kind, local + bit * rows + row]))
        return [pltpu.make_async_copy(a, b, in_sems.at[i]) for i, (a, b) in enumerate(copies)]

    def acc_copy(store):
        copies = []
        for kind in range(2):
            for block in range(local):
                index = kind * local + block
                far = acc_hbm if store else prior
                ends = (acc.at[kind, block], far.at[kind, block])
                ends = ends if store else ends[::-1]
                copies.append(pltpu.make_async_copy(*ends, acc_sems.at[index]))
        return copies

    def out_copy(bit, kind):
        far = outs[2 * bit + kind].at[0] if apart else outs[bit].at[kind]
        return pltpu.make_async_copy(stage.at[bit, kind], far, out_sems.at[2 * bit + kind])

    @pl.when(step == 0)
    def _():
        for copy in loads():
            copy.start()
        if has_prior:
            for copy in acc_copy(False):
                copy.start()
        start = local if has_prior else 0
        tokens = acc.shape[2]
        for kind in range(2):

            @pl.loop(start, acc.shape[1])
            def _(slot):
                acc[kind, slot] = jnp.zeros((tokens, width), jnp.float32)

        if has_prior:
            for copy in acc_copy(False):
                copy.wait()
        for copy in loads():
            copy.wait()

    first_slot = slots_ref[step]
    second_slot = slots_ref[pl.num_programs(0) + step]
    slots = (first_slot, second_slot)
    pre_act = dot_nn(cand[0, first_slot], up_ref[0, 0]) + dot_nn(cand[0, second_slot], up_ref[1, 0])
    value, slope = gelu_pair(pre_act)
    activated = value.astype(jnp.bfloat16)
    hidden_grad = dot_nt(cand[1, first_slot], down_ref[0, 0])
    hidden_grad = hidden_grad + dot_nt(cand[1, second_slot], down_ref[1, 0])
    pre_grad = (hidden_grad * slope).astype(jnp.bfloat16)
    parity = parity_ref[0]
    piece = width // (2 * halves)
    for index, slot in enumerate(slots):
        acc[0, slot] += dot_nn(activated, down_ref[index, 0])
        acc[1, slot] += dot_nt(pre_grad, up_ref[index, 0])
        for which, grad in enumerate(
            (dot_tn(cand[0, slot], pre_grad), dot_tn(activated, cand[1, slot]))
        ):
            square[which] = grad
            for half in range(halves):
                own = pl.multiple_of((2 * half + parity) * piece, piece)
                other = pl.multiple_of((2 * half + 1 - parity) * piece, piece)
                keep_ref[0, half, which, index] = square[which, pl.ds(own, piece), :]
                send_ref[0, half, which, index] = square[which, pl.ds(other, piece), :]

    @pl.when(step == last)
    def _():
        for copy in acc_copy(True):
            copy.start()
        order = [(bit, kind) for bit in range(bits) for kind in range(2)]
        for bit, kind in order:
            for row in range(rows):
                total = acc[kind, local + bit * rows + row]
                stage[bit, kind, :, pl.ds(row * width, width)] = total.astype(jnp.bfloat16)
            out_copy(bit, kind).start()
        for bit, kind in order:
            out_copy(bit, kind).wait()
        for copy in acc_copy(True):
            copy.wait()


def main_call(start, rows, slots, parity, inputs, out_grad, arrived, prior, w_up, w_down, halves, apart):
    tokens, features = inputs.shape
    slot_kinds, columns, width, _ = w_up.shape
    local = features // width
    came_apart = arrived[0].shape[0] == 1
    bits = len(arrived) // (1 + int(came_apart))
    cols = columns * rows // local
    slot_count = local + bits * rows
    first = start * columns // local
    has_prior = prior is not None
    piece = width // (2 * halves)
    dims = (local, bits, rows, width, slot_count, halves, first, has_prior, apart, came_apart)
    sends = bits * (1 + int(apart))
    anywhere = pl.BlockSpec(memory_space=pl.ANY)
    weight = pl.BlockSpec((slot_kinds, 1, width, width), lambda i, *_: (0, first + i, 0, 0))
    grad_block = pl.BlockSpec((1, halves, 2, slot_kinds, piece, width), lambda i, *_: (i, 0, 0, 0, 0, 0))
    grad_shape = jax.ShapeDtypeStruct((cols, halves, 2, slot_kinds, piece, width), jnp.float32)
    operands = [inputs, out_grad, *arrived] + ([prior] if has_prior else []) + [w_up, w_down]
    pair_flops = 2 * tokens * width * width * 6
    moved = 2 * cols * slot_kinds * width * width * 6 + 12 * tokens * width * slot_count
    return pl.pallas_call(
        functools.partial(main_body, dims),
        grid_spec=pltpu.PrefetchScalarGridSpec(
            num_scalar_prefetch=2,
            grid=(cols,),
            in_specs=[anywhere] * (len(operands) - 2) + [weight, weight],
            out_specs=[anywhere] * (1 + sends) + [grad_block, grad_block],
            scratch_shapes=[
                pltpu.VMEM((2, slot_count, tokens, width), jnp.bfloat16),
                pltpu.VMEM((2, slot_count, tokens, width), jnp.float32),
                pltpu.VMEM((bits, 2, tokens, rows * width), jnp.bfloat16),
                pltpu.VMEM((2, width, width), jnp.float32),
                pltpu.SemaphoreType.DMA((2 * slot_count,)),
                pltpu.SemaphoreType.DMA((2 * local,)),
                pltpu.SemaphoreType.DMA((2 * bits,)),
            ],
        ),
        out_shape=[
            jax.ShapeDtypeStruct((2, local, tokens, width), jnp.float32),
            *[jax.ShapeDtypeStruct((2 * bits // sends, tokens, rows * width), jnp.bfloat16)] * sends,
            grad_shape,
            grad_shape,
        ],
        cost_estimate=pl.CostEstimate(
            flops=pair_flops * cols * slot_kinds,
            bytes_accessed=moved,
            transcendentals=2 * cols * tokens * width,
        ),
        compiler_params=pltpu.CompilerParams(
            dimension_semantics=("arbitrary",), vmem_limit_bytes=60 << 20
        ),
        name="columns",
    )(slots, parity, *operands)


def halve_body(parity_ref, keep_ref, recv_ref, kept_ref, send_ref):
    parity = parity_ref[0]
    for half in range(kept_ref.shape[1]):
        own = 2 * half + parity
        other = 2 * half + 1 - parity
        kept_ref[:, half] = keep_ref[:, own] + recv_ref[:, own]
        send_ref[:, half] = keep_ref[:, other] + recv_ref[:, other]


def halve_call(per_row, parity, keep, recv):
    cols, halves, pair, slot_kinds, piece, width = keep.shape
    block = per_row
    spec = pl.BlockSpec((block, halves, pair, slot_kinds, piece, width), lambda i, *_: (i, 0, 0, 0, 0, 0))
    half_shape = (cols, halves // 2, pair, slot_kinds, piece, width)
    half_spec = pl.BlockSpec((block,) + half_shape[1:], lambda i, *_: (i, 0, 0, 0, 0, 0))
    return pl.pallas_call(
        halve_body,
        grid_spec=pltpu.PrefetchScalarGridSpec(
            num_scalar_prefetch=1,
            grid=(cols // block,),
            in_specs=[spec, spec],
            out_specs=[half_spec, half_spec],
        ),
        out_shape=[jax.ShapeDtypeStruct(half_shape, jnp.float32)] * 2,
        cost_estimate=pl.CostEstimate(flops=keep.size, bytes_accessed=12 * keep.size, transcendentals=0),
        name="halve",
    )(parity, keep, recv)


def grads_body(keep_ref, recv_ref, *refs):
    up_ref, down_ref = refs[-2], refs[-1]
    for which, ref in enumerate((up_ref, down_ref)):
        for slot in range(ref.shape[0]):
            ref[slot] = keep_ref[:, 0, which, slot] + recv_ref[:, 0, which, slot]


def grads_call(start, per_row, columns, keep, recv, prior):
    cols, _, pair, slot_kinds, piece, width = keep.shape
    block = per_row
    first = start
    spec = pl.BlockSpec((block, 1, pair, slot_kinds, piece, width), lambda i: (i, 0, 0, 0, 0, 0))
    out_spec = pl.BlockSpec((slot_kinds, block, piece, width), lambda i: (0, first + i, 0, 0))
    out_shape = jax.ShapeDtypeStruct((slot_kinds, columns, piece, width), jnp.float32)
    return pl.pallas_call(
        grads_body,
        grid=(cols // block,),
        in_specs=[spec, spec] + [pl.BlockSpec(memory_space=pl.ANY)] * len(prior),
        out_specs=[out_spec, out_spec],
        out_shape=[out_shape, out_shape],
        input_output_aliases={2 + i: i for i in range(len(prior))},
        cost_estimate=pl.CostEstimate(flops=keep.size, bytes_accessed=12 * keep.size, transcendentals=0),
        name="grads",
    )(keep, recv, *prior)


def total_body(bits, kinds, acc_ref, *refs):
    out_refs = refs[-kinds:]
    for kind in range(kinds):
        total = acc_ref[kind, 0]
        for bit in range(bits):
            total = total + refs[bit][kind].astype(jnp.float32)
        out_refs[kind][...] = total.astype(jnp.bfloat16)


def total_call(start, rows, first_kind, acc, arrived, prior):
    _, local, tokens, width = acc.shape
    bits = len(arrived)
    kinds = arrived[0].shape[0]
    tile = tokens // 2
    acc_spec = pl.BlockSpec((kinds, 1, tile, width), lambda i, t: (first_kind, start + i, t, 0))
    recv_spec = pl.BlockSpec((kinds, tile, width), lambda i, t: (0, t, i))
    out_spec = pl.BlockSpec((tile, width), lambda i, t: (t, start + i))
    out_shape = jax.ShapeDtypeStruct((tokens, local * width), jnp.bfloat16)
    size = kinds * rows * tokens * width
    return pl.pallas_call(
        functools.partial(total_body, bits, kinds),
        grid=(rows, 2),
        in_specs=[acc_spec] + [recv_spec] * bits + [pl.BlockSpec(memory_space=pl.ANY)] * len(prior),
        out_specs=[out_spec] * kinds,
        out_shape=[out_shape] * kinds,
        input_output_aliases={1 + bits + i: i for i in range(len(prior))},
        cost_estimate=pl.CostEstimate(flops=size * bits, bytes_accessed=(6 + 2 * bits) * size, transcendentals=0),
        name="totals",
    )(acc, *arrived, *prior)


def last_total(start, rows, acc, arrived, whole):
    _, _, width = acc.shape
    for row in range(rows):
        lanes = slice(row * width, (row + 1) * width)
        total = acc[start + row]
        for value in arrived:
            total = total + value[0, :, lanes].astype(jnp.float32)
        whole = lax.dynamic_update_slice(whole, total.astype(whole.dtype), (0, (start + row) * width))
    return whole


def shards(inputs, out_grad, w_up, w_down, partners):
    _, features = inputs.shape
    _, columns, width, _ = w_up.shape
    local = features // width
    bits = lax.axis_size("mp").bit_length() - 1
    dp_bits = lax.axis_size("dp").bit_length() - 1
    sizes = row_groups(local)
    starts = [sum(sizes[:group]) for group in range(len(sizes))]
    per_row = columns // local
    last = len(sizes) - 1
    device = lax.axis_index("mp")
    dp_index = lax.axis_index("dp")

    distance = jnp.bitwise_xor(partners // local, device)
    within = partners % local
    level = jnp.zeros_like(distance)
    for bit in range(1, bits):
        level = level + (distance >= 1 << bit).astype(jnp.int32)
    is_local = distance == 0
    parities = [(dp_index // 2**bit % 2).reshape(1).astype(jnp.int32) for bit in range(dp_bits)]

    arrived = []
    for group, (start, rows) in enumerate(zip(starts, sizes)):
        if group == 0:
            parts = []
            for kind, array in enumerate((inputs, out_grad)):
                if kind == 0:
                    block = array[None, :, start * width : (start + rows) * width]
                else:
                    block = pack_call(start, rows, width, array)
                sent = []
                for bit in range(bits):
                    sent.append(partner(block, "mp", bit))
                parts.append(sent)
            arrived.append([parts[kind][bit] for bit in range(bits) for kind in range(2)])
        else:
            pair = pack_call(start, rows, width, inputs, out_grad)
            arrived.append([partner(pair, "mp", bit) for bit in range(bits)])

    acc = None
    returned = []
    kept = []
    for group, (start, rows) in enumerate(zip(starts, sizes)):
        slot = jnp.where(is_local, within, local + level * rows + within - start)
        slots = slot[:, start * per_row : (start + rows) * per_row].reshape(-1)
        acc, *rest = main_call(
            start, rows, slots, parities[0], inputs, out_grad, arrived[group], acc, w_up, w_down,
            2 ** (dp_bits - 1), group == last,
        )
        sends = rest[:-2]
        keep, send = rest[-2:]
        if group == last:
            parts = []
            for kind in range(2):
                parts.append([partner(sends[2 * bit + kind], "mp", bit) for bit in range(bits)])
            returned.append(parts)
        else:
            returned.append([partner(sends[bit], "mp", bit) for bit in range(bits)])
        for bit in range(1, dp_bits):
            recv = partner(send, "dp", bit - 1)
            keep, send = halve_call(per_row, parities[bit], keep, recv)
        kept.append((keep, partner(send, "dp", dp_bits - 1)))

    grads = []
    for group, start in enumerate(starts):
        grads = grads_call(start, per_row, columns, *kept[group], grads)
    totals = []
    for group, (start, rows) in enumerate(zip(starts[:-1], sizes[:-1])):
        totals = total_call(start, rows, 0, acc, returned[group], totals)
    ends = []
    for kind in range(2):
        if kind == 0:
            ends += total_call(starts[-1], sizes[-1], kind, acc, returned[-1][kind], totals[:1])
        else:
            ends.append(last_total(starts[-1], sizes[-1], acc[kind], returned[-1][kind], totals[kind]))
    return (*ends, *grads)


def solution(mesh):
    in_specs = (
        P("dp", "mp"),
        P("dp", "mp"),
        P(None, "mp", None, None),
        P(None, "mp", None, None),
        P(None, "mp"),
    )
    out_specs = (P("dp", "mp"), P("dp", "mp"), P(None, "mp", "dp", None), P(None, "mp", "dp", None))

    return jax.shard_map(shards, mesh=mesh, in_specs=in_specs, out_specs=out_specs, check_vma=False)
```

```python
import functools

import jax
import jax.numpy as jnp
from jax import lax
from jax.experimental import pallas as pl
from jax.experimental.pallas import tpu as pltpu
from jax.sharding import PartitionSpec as P


def row_groups(local):
    edge = max(1, local // 8)
    middle = local - 2 * edge
    sizes = [edge, middle - middle // 3, middle // 3, edge] if middle >= 0 else [local]
    return [size for size in sizes if size > 0]


def partner(value, axis, distance):
    mask = 2**distance
    pairs = [(source, source ^ mask) for source in range(lax.axis_size(axis))]
    return lax.ppermute(value, axis, pairs)


def partners_of(values):
    arrived = []
    for bit, value in enumerate(values):
        arrived.append(partner(value, "mp", bit))
    return arrived


def gelu_pair(hidden):
    erf_part = lax.erf(hidden * 0.7071067811865476)
    value = 0.5 * hidden * (1.0 + erf_part)
    slope = 0.5 * (1.0 + erf_part) + hidden * jnp.exp(-0.5 * hidden * hidden) * 0.3989422804014327
    return value, slope


def dot_nn(left, right):
    return lax.dot_general(left, right, (((1,), (0,)), ((), ())), preferred_element_type=jnp.float32)


def dot_nt(left, right):
    return lax.dot_general(left, right, (((1,), (1,)), ((), ())), preferred_element_type=jnp.float32)


def dot_tn(left, right):
    return lax.dot_general(left, right, (((0,), (0,)), ((), ())), preferred_element_type=jnp.float32)


def pack_body(*refs):
    pair_ref = refs[-1]
    for kind, ref in enumerate(refs[:-1]):
        pair_ref[kind] = ref[...]


def pack_call(start, rows, width, *arrays):
    tokens = arrays[0].shape[0]
    kinds = len(arrays)
    column = pl.BlockSpec((tokens, width), lambda i: (0, start + i))
    size = kinds * tokens * rows * width
    return pl.pallas_call(
        pack_body,
        grid=(rows,),
        in_specs=[column] * kinds,
        out_specs=pl.BlockSpec((kinds, tokens, width), lambda i: (0, 0, i)),
        out_shape=jax.ShapeDtypeStruct((kinds, tokens, rows * width), arrays[0].dtype),
        cost_estimate=pl.CostEstimate(flops=0, bytes_accessed=4 * size, transcendentals=0),
        name="pack",
    )(*arrays)


def main_body(dims, slots_ref, parity_ref, *refs):
    local, bits, rows, width, _, halves, _, has_prior, apart, came_apart = dims
    x_hbm, g_hbm = refs[0], refs[1]
    arrived = refs[2 : 2 + bits * (1 + int(came_apart))]
    at = 2 + len(arrived)
    prior = refs[at] if has_prior else None
    at += int(has_prior)
    up_ref, down_ref = refs[at], refs[at + 1]
    acc_hbm = refs[at + 2]
    outs = refs[at + 3 : at + 3 + bits * (1 + int(apart))]
    at += 3 + len(outs)
    keep_ref, send_ref = refs[at], refs[at + 1]
    cand, acc, stage, square, in_sems, acc_sems, out_sems = refs[at + 2 :]
    step = pl.program_id(0)
    last = pl.num_programs(0) - 1

    def loads():
        copies = []
        for kind, source in enumerate((x_hbm, g_hbm)):
            for block in range(local):
                view = source.at[:, pl.ds(block * width, width)]
                copies.append((view, cand.at[kind, block]))
        for kind in range(2):
            for bit in range(bits):
                for row in range(rows):
                    whole = arrived[2 * bit + kind].at[0] if came_apart else arrived[bit].at[kind]
                    view = whole.at[:, pl.ds(row * width, width)]
                    copies.append((view, cand.at[kind, local + bit * rows + row]))
        return [pltpu.make_async_copy(a, b, in_sems.at[i]) for i, (a, b) in enumerate(copies)]

    def acc_copy(store):
        copies = []
        for kind in range(2):
            for block in range(local):
                index = kind * local + block
                far = acc_hbm if store else prior
                ends = (acc.at[kind, block], far.at[kind, block])
                ends = ends if store else ends[::-1]
                copies.append(pltpu.make_async_copy(*ends, acc_sems.at[index]))
        return copies

    def out_copy(bit, kind):
        far = outs[2 * bit + kind].at[0] if apart else outs[bit].at[kind]
        return pltpu.make_async_copy(stage.at[bit, kind], far, out_sems.at[2 * bit + kind])

    @pl.when(step == 0)
    def _():
        for copy in loads():
            copy.start()
        if has_prior:
            for copy in acc_copy(False):
                copy.start()
        start = local if has_prior else 0
        tokens = acc.shape[2]
        for kind in range(2):

            @pl.loop(start, acc.shape[1])
            def _(slot):
                acc[kind, slot] = jnp.zeros((tokens, width), jnp.float32)

        if has_prior:
            for copy in acc_copy(False):
                copy.wait()
        for copy in loads():
            copy.wait()

    first_slot = slots_ref[step]
    second_slot = slots_ref[pl.num_programs(0) + step]
    slots = (first_slot, second_slot)
    pre_act = dot_nn(cand[0, first_slot], up_ref[0, 0]) + dot_nn(cand[0, second_slot], up_ref[1, 0])
    value, slope = gelu_pair(pre_act)
    activated = value.astype(jnp.bfloat16)
    hidden_grad = dot_nt(cand[1, first_slot], down_ref[0, 0])
    hidden_grad = hidden_grad + dot_nt(cand[1, second_slot], down_ref[1, 0])
    pre_grad = (hidden_grad * slope).astype(jnp.bfloat16)
    parity = parity_ref[0]
    piece = width // (2 * halves)
    for index, slot in enumerate(slots):
        acc[0, slot] += dot_nn(activated, down_ref[index, 0])
        acc[1, slot] += dot_nt(pre_grad, up_ref[index, 0])
        for which, grad in enumerate(
            (dot_tn(cand[0, slot], pre_grad), dot_tn(activated, cand[1, slot]))
        ):
            square[which] = grad
            for half in range(halves):
                own = pl.multiple_of((2 * half + parity) * piece, piece)
                other = pl.multiple_of((2 * half + 1 - parity) * piece, piece)
                keep_ref[0, half, which, index] = square[which, pl.ds(own, piece), :]
                send_ref[0, half, which, index] = square[which, pl.ds(other, piece), :]

    @pl.when(step == last)
    def _():
        for copy in acc_copy(True):
            copy.start()
        order = [(bit, kind) for bit in range(bits) for kind in range(2)]
        for bit, kind in order:
            for row in range(rows):
                total = acc[kind, local + bit * rows + row]
                stage[bit, kind, :, pl.ds(row * width, width)] = total.astype(jnp.bfloat16)
            out_copy(bit, kind).start()
        for bit, kind in order:
            out_copy(bit, kind).wait()
        for copy in acc_copy(True):
            copy.wait()


def main_call(start, rows, slots, parity, inputs, out_grad, arrived, prior, w_up, w_down, halves, apart):
    tokens, features = inputs.shape
    slot_kinds, columns, width, _ = w_up.shape
    local = features // width
    came_apart = arrived[0].shape[0] == 1
    bits = len(arrived) // (1 + int(came_apart))
    cols = columns * rows // local
    slot_count = local + bits * rows
    first = start * columns // local
    has_prior = prior is not None
    piece = width // (2 * halves)
    dims = (local, bits, rows, width, slot_count, halves, first, has_prior, apart, came_apart)
    sends = bits * (1 + int(apart))
    anywhere = pl.BlockSpec(memory_space=pl.ANY)
    weight = pl.BlockSpec((slot_kinds, 1, width, width), lambda i, *_: (0, first + i, 0, 0))
    grad_block = pl.BlockSpec((1, halves, 2, slot_kinds, piece, width), lambda i, *_: (i, 0, 0, 0, 0, 0))
    grad_shape = jax.ShapeDtypeStruct((cols, halves, 2, slot_kinds, piece, width), jnp.float32)
    operands = [inputs, out_grad, *arrived] + ([prior] if has_prior else []) + [w_up, w_down]
    pair_flops = 2 * tokens * width * width * 6
    moved = 2 * cols * slot_kinds * width * width * 6 + 12 * tokens * width * slot_count
    return pl.pallas_call(
        functools.partial(main_body, dims),
        grid_spec=pltpu.PrefetchScalarGridSpec(
            num_scalar_prefetch=2,
            grid=(cols,),
            in_specs=[anywhere] * (len(operands) - 2) + [weight, weight],
            out_specs=[anywhere] * (1 + sends) + [grad_block, grad_block],
            scratch_shapes=[
                pltpu.VMEM((2, slot_count, tokens, width), jnp.bfloat16),
                pltpu.VMEM((2, slot_count, tokens, width), jnp.float32),
                pltpu.VMEM((bits, 2, tokens, rows * width), jnp.bfloat16),
                pltpu.VMEM((2, width, width), jnp.float32),
                pltpu.SemaphoreType.DMA((2 * slot_count,)),
                pltpu.SemaphoreType.DMA((2 * local,)),
                pltpu.SemaphoreType.DMA((2 * bits,)),
            ],
        ),
        out_shape=[
            jax.ShapeDtypeStruct((2, local, tokens, width), jnp.float32),
            *[jax.ShapeDtypeStruct((2 * bits // sends, tokens, rows * width), jnp.bfloat16)] * sends,
            grad_shape,
            grad_shape,
        ],
        cost_estimate=pl.CostEstimate(
            flops=pair_flops * cols * slot_kinds,
            bytes_accessed=moved,
            transcendentals=2 * cols * tokens * width,
        ),
        compiler_params=pltpu.CompilerParams(
            dimension_semantics=("arbitrary",), vmem_limit_bytes=60 << 20
        ),
        name="columns",
    )(slots, parity, *operands)


def halve_body(parity_ref, keep_ref, recv_ref, kept_ref, send_ref):
    parity = parity_ref[0]
    for half in range(kept_ref.shape[1]):
        own = 2 * half + parity
        other = 2 * half + 1 - parity
        kept_ref[:, half] = keep_ref[:, own] + recv_ref[:, own]
        send_ref[:, half] = keep_ref[:, other] + recv_ref[:, other]


def halve_call(per_row, parity, keep, recv):
    cols, halves, pair, slot_kinds, piece, width = keep.shape
    block = per_row
    spec = pl.BlockSpec((block, halves, pair, slot_kinds, piece, width), lambda i, *_: (i, 0, 0, 0, 0, 0))
    half_shape = (cols, halves // 2, pair, slot_kinds, piece, width)
    half_spec = pl.BlockSpec((block,) + half_shape[1:], lambda i, *_: (i, 0, 0, 0, 0, 0))
    return pl.pallas_call(
        halve_body,
        grid_spec=pltpu.PrefetchScalarGridSpec(
            num_scalar_prefetch=1,
            grid=(cols // block,),
            in_specs=[spec, spec],
            out_specs=[half_spec, half_spec],
        ),
        out_shape=[jax.ShapeDtypeStruct(half_shape, jnp.float32)] * 2,
        cost_estimate=pl.CostEstimate(flops=keep.size, bytes_accessed=12 * keep.size, transcendentals=0),
        name="halve",
    )(parity, keep, recv)


def grads_body(keep_ref, recv_ref, *refs):
    up_ref, down_ref = refs[-2], refs[-1]
    for which, ref in enumerate((up_ref, down_ref)):
        for slot in range(ref.shape[0]):
            ref[slot] = keep_ref[:, 0, which, slot] + recv_ref[:, 0, which, slot]


def grads_call(start, per_row, columns, keep, recv, prior):
    cols, _, pair, slot_kinds, piece, width = keep.shape
    block = per_row
    first = start
    spec = pl.BlockSpec((block, 1, pair, slot_kinds, piece, width), lambda i: (i, 0, 0, 0, 0, 0))
    out_spec = pl.BlockSpec((slot_kinds, block, piece, width), lambda i: (0, first + i, 0, 0))
    out_shape = jax.ShapeDtypeStruct((slot_kinds, columns, piece, width), jnp.float32)
    return pl.pallas_call(
        grads_body,
        grid=(cols // block,),
        in_specs=[spec, spec] + [pl.BlockSpec(memory_space=pl.ANY)] * len(prior),
        out_specs=[out_spec, out_spec],
        out_shape=[out_shape, out_shape],
        input_output_aliases={2 + i: i for i in range(len(prior))},
        cost_estimate=pl.CostEstimate(flops=keep.size, bytes_accessed=12 * keep.size, transcendentals=0),
        name="grads",
    )(keep, recv, *prior)


def total_body(bits, kinds, acc_ref, *refs):
    out_refs = refs[-kinds:]
    for kind in range(kinds):
        total = acc_ref[kind, 0]
        for bit in range(bits):
            total = total + refs[bit][kind].astype(jnp.float32)
        out_refs[kind][...] = total.astype(jnp.bfloat16)


def total_call(start, rows, first_kind, acc, arrived, prior):
    _, local, tokens, width = acc.shape
    bits = len(arrived)
    kinds = arrived[0].shape[0]
    tile = tokens // 2
    acc_spec = pl.BlockSpec((kinds, 1, tile, width), lambda i, t: (first_kind, start + i, t, 0))
    recv_spec = pl.BlockSpec((kinds, tile, width), lambda i, t: (0, t, i))
    out_spec = pl.BlockSpec((tile, width), lambda i, t: (t, start + i))
    out_shape = jax.ShapeDtypeStruct((tokens, local * width), jnp.bfloat16)
    size = kinds * rows * tokens * width
    return pl.pallas_call(
        functools.partial(total_body, bits, kinds),
        grid=(rows, 2),
        in_specs=[acc_spec] + [recv_spec] * bits + [pl.BlockSpec(memory_space=pl.ANY)] * len(prior),
        out_specs=[out_spec] * kinds,
        out_shape=[out_shape] * kinds,
        input_output_aliases={1 + bits + i: i for i in range(len(prior))},
        cost_estimate=pl.CostEstimate(flops=size * bits, bytes_accessed=(6 + 2 * bits) * size, transcendentals=0),
        name="totals",
    )(acc, *arrived, *prior)


def last_total(start, rows, acc, arrived, whole):
    _, _, width = acc.shape
    for row in range(rows):
        lanes = slice(row * width, (row + 1) * width)
        total = acc[start + row] + arrived[0][0, :, lanes].astype(jnp.float32)
        total = lax.optimization_barrier(total)
        for value in arrived[1:]:
            total = total + value[0, :, lanes].astype(jnp.float32)
        whole = lax.dynamic_update_slice(whole, total.astype(whole.dtype), (0, (start + row) * width))
    return whole


def shards(inputs, out_grad, w_up, w_down, partners):
    _, features = inputs.shape
    _, columns, width, _ = w_up.shape
    local = features // width
    bits = lax.axis_size("mp").bit_length() - 1
    dp_bits = lax.axis_size("dp").bit_length() - 1
    sizes = row_groups(local)
    starts = [sum(sizes[:group]) for group in range(len(sizes))]
    per_row = columns // local
    last = len(sizes) - 1
    device = lax.axis_index("mp")
    dp_index = lax.axis_index("dp")

    distance = jnp.bitwise_xor(partners // local, device)
    within = partners % local
    level = jnp.zeros_like(distance)
    for bit in range(1, bits):
        level = level + (distance >= 1 << bit).astype(jnp.int32)
    is_local = distance == 0
    parities = [(dp_index // 2**bit % 2).reshape(1).astype(jnp.int32) for bit in range(dp_bits)]

    arrived = []
    for group, (start, rows) in enumerate(zip(starts, sizes)):
        if group == 0:
            parts = []
            for kind, array in enumerate((inputs, out_grad)):
                if kind == 0:
                    block = array[None, :, start * width : (start + rows) * width]
                else:
                    block = pack_call(start, rows, width, array)
                parts.append(partners_of([block] * bits))
            arrived.append([parts[kind][bit] for bit in range(bits) for kind in range(2)])
        else:
            pair = pack_call(start, rows, width, inputs, out_grad)
            arrived.append(partners_of([pair] * bits))

    acc = None
    returned = []
    kept = []
    for group, (start, rows) in enumerate(zip(starts, sizes)):
        slot = jnp.where(is_local, within, local + level * rows + within - start)
        slots = slot[:, start * per_row : (start + rows) * per_row].reshape(-1)
        acc, *rest = main_call(
            start, rows, slots, parities[0], inputs, out_grad, arrived[group], acc, w_up, w_down,
            2 ** (dp_bits - 1), group == last,
        )
        sends = rest[:-2]
        keep, send = rest[-2:]
        if group == last:
            parts = []
            for kind in range(2):
                parts.append(partners_of(sends[kind::2]))
            returned.append(parts)
        else:
            returned.append(partners_of(sends))
        for bit in range(1, dp_bits):
            recv = partner(send, "dp", bit - 1)
            keep, send = halve_call(per_row, parities[bit], keep, recv)
        kept.append((keep, partner(send, "dp", dp_bits - 1)))

    grads = []
    for group, start in enumerate(starts):
        grads = grads_call(start, per_row, columns, *kept[group], grads)
    totals = []
    for group, (start, rows) in enumerate(zip(starts[:-1], sizes[:-1])):
        totals = total_call(start, rows, 0, acc, returned[group], totals)
    ends = []
    for kind in range(2):
        if kind == 0:
            ends += total_call(starts[-1], sizes[-1], kind, acc, returned[-1][kind], totals[:1])
        else:
            ends.append(last_total(starts[-1], sizes[-1], acc[kind], returned[-1][kind], totals[kind]))
    return (*ends, *grads)


def solution(mesh):
    in_specs = (
        P("dp", "mp"),
        P("dp", "mp"),
        P(None, "mp", None, None),
        P(None, "mp", None, None),
        P(None, "mp"),
    )
    out_specs = (P("dp", "mp"), P("dp", "mp"), P(None, "mp", "dp", None), P(None, "mp", "dp", None))

    return jax.shard_map(shards, mesh=mesh, in_specs=in_specs, out_specs=out_specs, check_vma=False)
```
